32 devices in a mesh: pb: 8 (over z, x), row: 4 (over y, core).
Axes of the slice: x: 2, y: 2, z: 4, core: 2. Of those that a mesh axis runs over, the one named last changes fastest.
Arguments:
- kernels: bfloat16 [8, 4096, 4096], P('pb', 'row'), may hold values from -6 to 6
- orbitals: bfloat16 [4096, 1024], P('pb'), may hold values from -0.75 to 0.75
- pairs: int32 [8, 4, 2], replicated, may hold values from 0 to 15
- k_slot: int32 [16], replicated, may hold values from 0 to 15, each once
- pair_count: int32 [8], replicated, may hold values from 1 to 4, as said below
Outputs:
- exchange_fields: float32 [4, 1024, 1024], P('row', 'pb')
The draws below stay inside these ranges and needn't reach their ends.
Inputs may be any that keep to these rules, and one draw needn't show every extreme that they name: `k_slot`: every slot holds exactly one k-point. pairs p < pair_count[q] are live; some transfer vector has all 4 live.
All inputs are finite; a program needn't handle non-finite values.
Results may differ from the reference program's by a relative error of at most 0.0029.
Values may be sent and summed in bfloat16 or wider, within the bound.
A program may use at most 128 MiB of HBM per device.

```python
import jax
import jax.numpy as jnp
from jax import lax

NMU = 4096
NORB = 64
NPAIR = 4
Q = 8
K = 16
N_ROW = 4


def draw_pair_count(key, part):
    first_key = jax.random.fold_in(key, 11)
    second_key = jax.random.fold_in(key, 23)
    counts = jax.random.randint(first_key, (Q,), 1, NPAIR + 1).astype(jnp.int32)
    full_index = jax.random.randint(second_key, (), 0, Q)
    return counts.at[full_index].set(NPAIR).astype(jnp.int32)


def place_ends(entries, key, low, top_value):
    index_at = [jax.random.randint(jax.random.fold_in(key, axis), (), 0, length) for axis, length in enumerate(entries.shape)]
    widest = entries.shape.index(max(entries.shape))
    beside = index_at[:widest] + [(index_at[widest] + 1) % entries.shape[widest]] + index_at[widest + 1:]
    return entries.at[tuple(index_at)].set(low).at[tuple(beside)].set(top_value)


def block_levels(stream_key, shape, split, smallest, high):
    factor_of, own = 1.0, jax.random.fold_in(stream_key, 6)
    for axis_at, blocks in split:
        heights = jnp.exp(jax.random.uniform(jax.random.fold_in(own, axis_at), (blocks,), jnp.float32, smallest / len(split), high / len(split)))
        factor_of = factor_of * jnp.repeat(heights, shape[axis_at] // blocks).reshape([-1 if axis == axis_at else 1 for axis in range(len(shape))])
    return factor_of


def scatter_about(own_key, dims, width, reach, cuts=(), held_as=jnp.bfloat16):
    drawn = jax.random.normal(own_key, dims, jnp.float32) * width
    if len(cuts) > 0:
        drawn = block_levels(own_key, dims, cuts, -0.22, 0.18) * drawn
    return jnp.clip(drawn, min=-reach, max=reach).astype(held_as)


def setup_inputs(seed: int = 0) -> dict:
    key_list = jax.random.split(jax.random.key(seed), 6)
    kernels = scatter_about(key_list[0], (Q, NMU, NMU), 1.0, 6.0, ((0, 8), (1, 4)))
    orbitals = scatter_about(key_list[1], (NMU, K * NORB), 0.125, 0.75, ((0, 8),))
    pairs = place_ends(jax.random.randint(key_list[2], (Q, NPAIR, 2), 0, K), jax.random.fold_in(key_list[2], 1), 0, K - 1).astype(jnp.int32)
    k_slot = jax.random.permutation(key_list[3], K).astype(jnp.int32)
    pair_count = draw_pair_count(jax.random.fold_in(key_list[5], 71), 0)
    return {"kernels": kernels, "orbitals": orbitals, "pairs": pairs, "k_slot": k_slot, "pair_count": pair_count}


def pair_fields(weight, orb_left, orb_right):
    wide_weight = weight.astype(jnp.float32)
    right_gram = jnp.dot(orb_right, orb_right.T, preferred_element_type=jnp.float32)
    first_term = jnp.dot((wide_weight * right_gram).astype(jnp.bfloat16), orb_left, preferred_element_type=jnp.float32)
    left_gram = jnp.dot(orb_left, orb_left.T, preferred_element_type=jnp.float32)
    second_hadamard = (wide_weight * left_gram).astype(jnp.bfloat16)
    second_term = jnp.dot(second_hadamard.T, orb_right, preferred_element_type=jnp.float32)
    return first_term, second_term


def reference(kernels, orbitals, pairs, k_slot, pair_count):
    orbital_cube = orbitals.reshape(NMU, K, NORB)

    def per_vector(field_sum, inputs):
        weight, pair_list, live_count = inputs
        for pair_index in range(NPAIR):
            k_left = pair_list[pair_index, 0]
            k_right = pair_list[pair_index, 1]
            orb_left = orbital_cube[:, k_slot[k_left], :]
            orb_right = orbital_cube[:, k_slot[k_right], :]
            first_term, second_term = pair_fields(weight, orb_left, orb_right)
            live_flag = jnp.where(pair_index < live_count, 1.0, 0.0).astype(jnp.float32)
            field_sum = field_sum.at[:, k_left, :].add(live_flag * first_term)
            field_sum = field_sum.at[:, k_right, :].add(live_flag * second_term)
        return field_sum, None

    start_sum = jnp.zeros((NMU, K, NORB), jnp.float32)
    field_sum, unused = lax.scan(per_vector, start_sum, (kernels, pairs, pair_count))
    return field_sum.reshape(N_ROW, NMU // N_ROW, K * NORB)
```

```python
import functools

import jax
import jax.numpy as jnp
from jax import lax
from jax.experimental import pallas as pl
from jax.experimental.pallas import tpu as pltpu
from jax.sharding import PartitionSpec as P

MESH = pl.DeviceIdType.MESH
BF16 = jnp.bfloat16
F32 = jnp.float32
NT = (((1,), (1,)), ((), ()))


def pick_kernel(width, pairs_ref, slot_ref, orb_ref, out_ref):
    pair_total, pb_count, piece, lanes = out_ref.shape
    rows = pl.ds(pl.multiple_of(lax.axis_index("row") * piece, piece), piece)
    low = lax.broadcasted_iota(jnp.int32, (piece, lanes), 1) < width

    def fetch(k, want):
        slot = slot_ref[k]
        block = orb_ref[rows, pl.ds(pl.multiple_of((slot >> 1) * lanes, lanes), lanes)].astype(F32)
        moved = pltpu.roll(block, width, 1)
        return jnp.where((slot & 1) == want, block, moved)

    def step(q, carry):
        for p in range(pair_total):
            left = fetch(pairs_ref[q, p, 0], 0)
            right = fetch(pairs_ref[q, p, 1], 1)
            out_ref[p, q] = jnp.where(low, left, right).astype(BF16)
        return carry

    lax.fori_loop(0, pb_count, step, 0)


def main_kernel(dims, picked, kern, out, w, basis, rows_r, rows_l, rows_t, f1, f2s, f2r, cbuf,
                w_sem, d_send, d_recv, g_send, g_recv, h_send, h_recv, y_send, y_recv,
                s_send, s_recv, c_send, c_recv):
    pb_count, row_devices, pair_total, piece, width = dims
    pb, row = lax.axis_index("pb"), lax.axis_index("row")
    chips = row_devices // 2
    part, chip = lax.rem(row, 2), lax.div(row, 2)
    mate = row + 1 - 2 * part
    row_count = w.shape[0]
    lanes = basis.shape[4]
    share = row_count // pb_count
    order = [(e, flip) for e in range(1, chips) for flip in (0, 1)] + [(0, 1), (0, 0)]

    def peer(e, flip):
        side = 1 - part if flip else part
        return 2 * lax.rem(chip + e, chips) + side

    w_copy = pltpu.make_async_copy(kern.at[0], w, w_sem)
    w_copy.start()

    barrier = pltpu.get_barrier_semaphore()

    def greet_pb(d, c):
        pl.semaphore_signal(barrier, inc=1, device_id=(lax.rem(pb + d, pb_count), row), device_id_type=MESH)
        return c

    def greet_row(d, c):
        pl.semaphore_signal(barrier, inc=1, device_id=(pb, lax.rem(row + d, row_devices)), device_id_type=MESH)
        return c

    lax.fori_loop(1, pb_count, greet_pb, 0)
    lax.fori_loop(1, row_devices, greet_row, 0)
    pl.semaphore_wait(barrier, pb_count + row_devices - 2)

    def spot(p, j, which):
        return basis.at[p, j, which]

    def points(p, r):
        span = pb_count // row_devices
        return basis[p, pl.ds(r * span, span)].reshape(row_count, lanes)

    def own(p):
        return pltpu.make_async_copy(picked.at[p, pb], spot(p, pb, row), d_recv.at[p, 0])

    def direct(p, d):
        q = lax.rem(pb + d, pb_count)
        return pltpu.make_async_remote_copy(
            src_ref=picked.at[p, q], dst_ref=spot(p, pb, row),
            send_sem=d_send.at[p, d], recv_sem=d_recv.at[p, d],
            device_id=(q, row), device_id_type=MESH)

    def across(p, e):
        block = basis.at[p, :, row]
        return pltpu.make_async_remote_copy(
            src_ref=block, dst_ref=block, send_sem=y_send.at[p, e - 1], recv_sem=y_recv.at[p, e - 1],
            device_id=(pb, peer(e, 0)), device_id_type=MESH)

    def to_mate(p):
        block = basis.at[p, :, row]
        return pltpu.make_async_remote_copy(
            src_ref=block, dst_ref=block, send_sem=g_send.at[p], recv_sem=g_recv.at[p],
            device_id=(pb, mate), device_id_type=MESH)

    def onward(p, e):
        block = basis.at[p, :, peer(chips - e, 0)]
        return pltpu.make_async_remote_copy(
            src_ref=block, dst_ref=block, send_sem=h_send.at[p, e - 1], recv_sem=h_recv.at[p, e - 1],
            device_id=(pb, mate), device_id_type=MESH)

    def shed(p, s):
        to = peer(*order[s])
        return pltpu.make_async_remote_copy(
            src_ref=f2s.at[p, s], dst_ref=f2r.at[p, s], send_sem=s_send.at[p, s], recv_sem=s_recv.at[p, s],
            device_id=(pb, to), device_id_type=MESH)

    def c_rows(j):
        return pl.ds(pl.multiple_of(j * share, share), share)

    def own_c(p):
        return pltpu.make_async_copy(cbuf.at[p, c_rows(pb)], out.at[p, pb], c_recv.at[p, 0])

    def give(p, d):
        j = lax.rem(pb + d, pb_count)
        return pltpu.make_async_remote_copy(
            src_ref=cbuf.at[p, c_rows(j)], dst_ref=out.at[p, pb], send_sem=c_send.at[p, d], recv_sem=c_recv.at[p, d],
            device_id=(j, row), device_id_type=MESH)

    def loop(low, high, body):
        def step(i, c):
            body(i)
            return c
        lax.fori_loop(low, high, step, 0)

    def send_pair(p):
        own(p).start()
        loop(1, pb_count, lambda d: direct(p, d).start())

    loop(0, pair_total, send_pair)

    def spread(p):
        own(p).wait()
        loop(1, pb_count, lambda d: direct(p, d).wait_recv())
        for e in range(1, chips):
            across(p, e).start()
        to_mate(p).start()

    def pass_far(p):
        for e in range(1, chips):
            across(p, e).wait_recv()
            onward(p, e).start()

    low = lax.broadcasted_iota(jnp.int32, (row_count, lanes), 1) < width

    def finish_pair(p):
        total = f2s[p, row_devices - 1].astype(F32)
        for s in range(row_devices - 1):
            shed(p, s).wait_recv()
            total = total + f2r[p, s].astype(F32)
        stacked = jnp.concatenate([jnp.zeros_like(total), total], axis=0)
        cbuf[p] = jnp.where(low, f1[p], stacked.T).astype(BF16)
        loop(1, pb_count, lambda d: give(p, d).start())
        own_c(p).start()

    def tile_of(p, s):
        to = peer(*order[s])
        cols = pl.ds(pl.multiple_of(to * row_count, row_count), row_count)
        there = points(p, to)
        second = None
        chunk = row_count // 2
        for m in range(2):
            here = slice(m * chunk, (m + 1) * chunk)
            weight = w[here, cols].astype(F32)
            gram = lax.dot_general(rows_r[here], there, NT, preferred_element_type=F32)
            first = jnp.dot((weight * gram).astype(BF16), there, preferred_element_type=F32)
            f1[p, here] = first if s == 0 else f1[p, here] + first
            gram = lax.dot_general(rows_l[here], there, NT, preferred_element_type=F32)
            term = jnp.dot(rows_t[:, here], (weight * gram).astype(BF16), preferred_element_type=F32)
            second = term if second is None else second + term
        f2s[p, s] = second[width:].astype(BF16)
        if s < row_devices - 1:
            shed(p, s).start()

    spread(0)
    pass_far(0)
    w_copy.wait()

    def pair_step(p):
        to_mate(p).wait_recv()
        for e in range(1, chips):
            onward(p, e).wait_recv()
        mine = points(p, row).astype(F32)
        rows_r[...] = jnp.where(low, 0, mine).astype(BF16)
        rows_l[...] = jnp.where(low, mine, 0).astype(BF16)
        rows_t[...] = mine.T.astype(BF16)
        for s in range(row_devices):
            tile_of(p, s)
            if s == 0:
                pl.when(p + 1 < pair_total)(lambda: spread(p + 1))
                pl.when(p > 0)(lambda: finish_pair(p - 1))
            if s == row_devices - 2:
                pl.when(p + 1 < pair_total)(lambda: pass_far(p + 1))

    loop(0, pair_total, pair_step)
    finish_pair(pair_total - 1)

    def settle(p):
        own_c(p).wait()

        to_mate(p).wait_send()
        for e in range(1, chips):
            across(p, e).wait_send()
            onward(p, e).wait_send()

        def one(d):
            direct(p, d).wait_send()
            give(p, d).wait()

        loop(1, pb_count, one)
        for s in range(row_devices - 1):
            shed(p, s).wait_send()

    loop(0, pair_total, settle)


def combine_kernel(width, pairs_ref, count_ref, got_ref, out_ref):
    pair_total, pb_count, share, lanes = got_ref.shape
    low = lax.broadcasted_iota(jnp.int32, (share, lanes), 1) < width
    out_ref[...] = jnp.zeros_like(out_ref)

    def step(q, carry):
        for p in range(pair_total):
            live = p < count_ref[q]
            block = jnp.where(live, got_ref[p, q].astype(F32), 0.0)
            moved = pltpu.roll(block, width, 1)
            for side in range(2):
                k = pairs_ref[q, p, side]
                odd = k & 1
                value = jnp.where(odd == side, block, moved)
                value = jnp.where(low == (odd == 0), value, 0.0)
                spot = pl.ds(pl.multiple_of((k >> 1) * lanes, lanes), lanes)
                out_ref[0, :, spot] += value
        return carry

    lax.fori_loop(0, pb_count, step, 0)


def plain_shards(kernels, orbitals, pairs, k_slot, pair_count):
    pb_count, row_devices = lax.axis_size("pb"), lax.axis_size("row")
    row_count, point_total = kernels.shape[1:]
    pair_total = pairs.shape[1]
    k_total = k_slot.shape[0]
    width = orbitals.shape[1] // k_total
    lanes = 2 * width
    piece = orbitals.shape[0] // row_devices
    far = max(row_devices // 2 - 1, 1)
    share = row_count // pb_count
    smem = pl.BlockSpec(memory_space=pltpu.SMEM)
    vmem = pl.BlockSpec(memory_space=pltpu.VMEM)
    hbm = pl.BlockSpec(memory_space=pl.ANY)
    picked = pl.pallas_call(
        functools.partial(pick_kernel, width),
        out_shape=jax.ShapeDtypeStruct((pair_total, pb_count, piece, lanes), BF16),
        in_specs=[smem, smem, vmem],
        out_specs=vmem,
    )(pairs, k_slot, orbitals)
    sems = pltpu.SemaphoreType.DMA
    got = pl.pallas_call(
        functools.partial(main_kernel, (pb_count, row_devices, pair_total, piece, width)),
        out_shape=jax.ShapeDtypeStruct((pair_total, pb_count, share, lanes), BF16),
        in_specs=[hbm, hbm],
        out_specs=hbm,
        scratch_shapes=[
            pltpu.VMEM((row_count, point_total), BF16),
            pltpu.VMEM((pair_total, pb_count, row_devices, piece, lanes), BF16),
            pltpu.VMEM((row_count, lanes), BF16),
            pltpu.VMEM((row_count, lanes), BF16),
            pltpu.VMEM((lanes, row_count), BF16),
            pltpu.VMEM((pair_total, row_count, lanes), F32),
            pltpu.VMEM((pair_total, row_devices, width, row_count), BF16),
            pltpu.VMEM((pair_total, row_devices, width, row_count), BF16),
            pltpu.VMEM((pair_total, row_count, lanes), BF16),
            sems,
            sems((pair_total, pb_count)),
            sems((pair_total, pb_count)),
            sems((pair_total,)),
            sems((pair_total,)),
            sems((pair_total, far)),
            sems((pair_total, far)),
            sems((pair_total, far)),
            sems((pair_total, far)),
            sems((pair_total, row_devices)),
            sems((pair_total, row_devices)),
            sems((pair_total, pb_count)),
            sems((pair_total, pb_count)),
        ],
        compiler_params=pltpu.CompilerParams(
            collective_id=0, has_side_effects=True, vmem_limit_bytes=56 * 1024 * 1024
        ),
    )(picked, kernels)
    return pl.pallas_call(
        functools.partial(combine_kernel, width),
        out_shape=jax.ShapeDtypeStruct((1, share, k_total * width), F32),
        in_specs=[smem, smem, vmem],
        out_specs=vmem,
    )(pairs, pair_count, got)


def swift_kernel(dims, pairs_ref, slot_ref, orb, kern, out, orb_v, orb_t, w, wt, picked, basis, rows_l, rows_r,
                 rows_p, nat_r, l1s, l1r, keep, l2s, l2r, cbuf, o_sem, w_sem, d_send, d_recv, x_send, x_recv,
                 g_send, g_recv, h_send, h_recv, a_send, a_recv, b_send, b_recv, c_send, c_recv):
    pb_count, pair_total, piece, width = dims
    pb, row = lax.axis_index("pb"), lax.axis_index("row")
    row_devices = basis.shape[1]
    row_count, point_total = w.shape
    span = pb_count // row_devices
    half = pb_count // 2
    share = row_count // pb_count
    part, chip = lax.rem(row, 2), lax.div(row, 2)
    side_x, side_z = lax.rem(pb, 2), lax.div(pb, 2)
    mate = row + 1 - 2 * part
    far = 2 * (1 - chip) + part
    bounds = [1, half, half + half // 2, pb_count]
    groups = range(3)

    def ahead(m):
        dz, dx = m // 2, m % 2
        return lax.rem(side_z + dz, half) * 2 + lax.rem(side_x + dx, 2)

    def slot_of(j):
        dz = lax.rem(side_z - j // 2 + half, half)
        return 2 * dz + lax.rem(side_x + j % 2, 2)

    def loop(low, high, body):
        def step(i, c):
            body(i)
            return c
        lax.fori_loop(low, high, step, 0)

    orb_copy = pltpu.make_async_copy(orb, orb_v, o_sem)
    orb_copy.start()
    w_copy = pltpu.make_async_copy(kern.at[0], w, w_sem)
    w_copy.start()

    barrier = pltpu.get_barrier_semaphore()
    loop(1, pb_count, lambda m: pl.semaphore_signal(
        barrier, inc=1, device_id=(lax.rem(pb + m, pb_count), row), device_id_type=MESH))
    pl.semaphore_signal(barrier, inc=1, device_id=(pb, mate), device_id_type=MESH)
    pl.semaphore_signal(barrier, inc=1, device_id=(pb, far), device_id_type=MESH)

    def direct(p, m):
        return pltpu.make_async_remote_copy(
            src_ref=picked.at[p, m], dst_ref=basis.at[p, row, m], send_sem=d_send.at[p, m], recv_sem=d_recv.at[p, m],
            device_id=(ahead(m), row), device_id_type=MESH)

    def passed(p, g, quarter, to, send, recv):
        block = basis.at[p, quarter, pl.ds(bounds[g], bounds[g + 1] - bounds[g])]
        return pltpu.make_async_remote_copy(
            src_ref=block, dst_ref=block, send_sem=send.at[p, g], recv_sem=recv.at[p, g],
            device_id=(pb, to), device_id_type=MESH)

    def across(p, g):
        return passed(p, g, row, far, x_send, x_recv)

    def to_mate(p, g):
        return passed(p, g, row, mate, g_send, g_recv)

    def onward(p, g):
        return passed(p, g, far, mate, h_send, h_recv)

    def fold(p, i):
        return pltpu.make_async_remote_copy(
            src_ref=l1s.at[p, i], dst_ref=l1r.at[p, i], send_sem=a_send.at[p, i], recv_sem=a_recv.at[p, i],
            device_id=(pb, mate), device_id_type=MESH)

    def shed(p):
        return pltpu.make_async_remote_copy(
            src_ref=l2s.at[p], dst_ref=l2r.at[p], send_sem=b_send.at[p], recv_sem=b_recv.at[p],
            device_id=(pb, far), device_id_type=MESH)

    def give(p, side, m):
        return pltpu.make_async_remote_copy(
            src_ref=cbuf.at[p, side, ahead(m)], dst_ref=out.at[p, side, pb],
            send_sem=c_send.at[p, side, m], recv_sem=c_recv.at[p, side, m],
            device_id=(ahead(m), row), device_id_type=MESH)

    def own_c(p, side):
        return pltpu.make_async_copy(cbuf.at[p, side, pb], out.at[p, side, pb], c_recv.at[p, side, 0])

    def take(quarter, k):
        return orb_t[quarter, slot_ref[k]]

    orb_copy.wait()

    def turn(r):
        block = orb_v[pl.ds(pl.multiple_of(r * piece, piece), piece), :].T
        orb_t[r] = block.reshape(orb_t.shape[1:])

    turn(row)

    def pick(p):
        def one(m):
            q = ahead(m)
            for side in range(2):
                picked[p, m, side * width:(side + 1) * width] = take(row, pairs_ref[p, side, q])
        loop(1, pb_count, one)

    def send(p):
        loop(1, pb_count, lambda m: direct(p, m).start())

    pick(0)
    pl.semaphore_wait(barrier, pb_count + 1)
    send(0)

    def pick_send(p):
        pick(p)
        send(p)

    loop(1, pair_total, pick_send)
    loop(1, row_devices, lambda e: turn(lax.rem(row + e, row_devices)))

    def own(p):
        def one(r):
            for side in range(2):
                basis[p, r, 0, side * width:(side + 1) * width] = take(r, pairs_ref[p, side, pb])
        loop(0, row_devices, one)

    loop(0, pair_total, own)

    def spread(p, g):
        for m in range(bounds[g], bounds[g + 1]):
            direct(p, m).wait_recv()
        across(p, g).start()
        to_mate(p, g).start()

    def pass_far(p, g):
        across(p, g).wait_recv()
        onward(p, g).start()

    def turn_w(i):
        cols = pl.ds(pl.multiple_of(i * row_count // 2, row_count // 2), row_count // 2)
        for b in range(pb_count):
            at = (b % 2) * half + b // 2
            wt[cols, at * share:(at + 1) * share] = w[b * share:(b + 1) * share, cols].T

    w_copy.wait()
    steps = point_total * 2 // row_count
    turn_w(0)
    spread(0, 0)
    loop(1, steps // 2, turn_w)
    spread(0, 1)
    loop(steps // 2, steps - 2, turn_w)
    spread(0, 2)
    pass_far(0, 0)
    loop(steps - 2, steps, turn_w)
    pass_far(0, 1)
    pass_far(0, 2)

    def tile_t(p, s, side):
        parts = []
        for i in range(span):
            m = slot_of(s * span + i)
            for r in range(row_devices):
                parts.append(basis[p, r, m, side * width:(side + 1) * width, :])
        return jnp.concatenate(parts, axis=1)

    def finish(p):
        fold(p, 1).wait_recv()
        shed(p).wait_recv()
        total = keep[p] + l1r[p, 1] + l2r[p].astype(F32)
        for j in range(pb_count):
            cbuf[p, 1, j] = total[:, j * share:(j + 1) * share].astype(BF16)
        loop(1, pb_count, lambda m: give(p, 1, m).start())
        own_c(p, 1).start()

    def column_tile(p, s):
        cols = pl.ds(pl.multiple_of(s * row_count, row_count), row_count)
        there_l, there_r = tile_t(p, s, 0), tile_t(p, s, 1)
        nat_r[s] = there_r.T
        total = None
        chunk = row_count // 2
        for m in range(2):
            here = slice(m * chunk, (m + 1) * chunk)
            gram = jnp.dot(rows_l[here], there_l, preferred_element_type=F32)
            term = jnp.dot(rows_r[:, here], (w[here, cols].astype(F32) * gram).astype(BF16), preferred_element_type=F32)
            total = term if total is None else total + term
        return total

    def row_tile(p, h, s):
        lanes = slice(h * row_count // 2, (h + 1) * row_count // 2)
        gram = jnp.dot(nat_r[s], rows_p[:, lanes], preferred_element_type=F32)
        rows = slice(s * row_count, (s + 1) * row_count)
        return jnp.dot(tile_t(p, s, 0), (wt[rows, lanes].astype(F32) * gram).astype(BF16), preferred_element_type=F32)

    def row_half(p, h, between):
        total = None
        for s in range(row_devices):
            term = row_tile(p, h, s)
            total = term if total is None else total + term
            between(s)
        for i in range(half):
            cbuf[p, 0, 2 * i + h] = total[:, i * share:(i + 1) * share].astype(BF16)
        for dz in range(1, half):
            give(p, 0, 2 * dz + lax.rem(side_x + h, 2)).start()
        pl.when(side_x != h)(lambda: give(p, 0, 1).start())
        pl.when(side_x == h)(lambda: own_c(p, 0).start())

    def pair_step(p):
        for g in groups:
            to_mate(p, g).wait_recv()
            onward(p, g).wait_recv()
        more = p + 1 < pair_total
        rows_l[...] = tile_t(p, row, 0).T
        right = tile_t(p, row, 1)
        rows_r[...] = right
        order = [b for h in range(2) for b in range(h, pb_count, 2)]
        rows_p[...] = jnp.concatenate([right[:, b * share:(b + 1) * share] for b in order], axis=1)

        l1s[p, 0] = column_tile(p, 2 * (1 - chip) + 1 - part)
        fold(p, 0).start()
        pl.when(more)(lambda: spread(p + 1, 0))
        there = column_tile(p, far)
        fold(p, 0).wait_recv()
        l2s[p] = (there + l1r[p, 0]).astype(BF16)
        shed(p).start()
        pl.when(more)(lambda: spread(p + 1, 1))
        l1s[p, 1] = column_tile(p, mate)
        fold(p, 1).start()
        pl.when(more)(lambda: spread(p + 1, 2))
        keep[p] = column_tile(p, row)
        pl.when(p > 0)(lambda: finish(p - 1))

        def first(s):
            if s == 2:
                pl.when(more)(lambda: pass_far(p + 1, 0))

        def second(s):
            if s == 0:
                pl.when(more)(lambda: pass_far(p + 1, 1))
            if s == 2:
                pl.when(more)(lambda: pass_far(p + 1, 2))

        row_half(p, 0, first)
        row_half(p, 1, second)

    loop(0, pair_total, pair_step)
    finish(pair_total - 1)

    def settle(p):
        for g in groups:
            across(p, g).wait_send()
            to_mate(p, g).wait_send()
            onward(p, g).wait_send()
        for i in range(2):
            fold(p, i).wait_send()
        shed(p).wait_send()
        loop(1, pb_count, lambda m: direct(p, m).wait_send())
        for side in range(2):
            own_c(p, side).wait()
            loop(1, pb_count, lambda m: give(p, side, m).wait())

    loop(0, pair_total, settle)


def swift_combine(pairs_ref, count_ref, got_ref, out_ref, total):
    pair_total, sides, pb_count, width, share = got_ref.shape
    total[...] = jnp.zeros_like(total)

    def step(q, carry):
        for p in range(pair_total):
            live = p < count_ref[q]
            for side in range(sides):
                k = pairs_ref[p, side, q]
                total[k] += jnp.where(live, got_ref[p, side, q].astype(F32), 0.0)
        return carry

    lax.fori_loop(0, pb_count, step, 0)
    out_ref[0] = total[...].reshape(total.shape[0] * width, share).T


def swift_shards(kernels, orbitals, pairs, k_slot, pair_count):
    pb_count, row_devices = lax.axis_size("pb"), lax.axis_size("row")
    row_count, point_total = kernels.shape[1:]
    pair_total = pairs.shape[1]
    k_total = k_slot.shape[0]
    width = orbitals.shape[1] // k_total
    piece = orbitals.shape[0] // row_devices
    share = row_count // pb_count
    pairs = jnp.transpose(pairs, (1, 2, 0))
    smem = pl.BlockSpec(memory_space=pltpu.SMEM)
    vmem = pl.BlockSpec(memory_space=pltpu.VMEM)
    hbm = pl.BlockSpec(memory_space=pl.ANY)
    sems = pltpu.SemaphoreType.DMA
    got = pl.pallas_call(
        functools.partial(swift_kernel, (pb_count, pair_total, piece, width)),
        out_shape=jax.ShapeDtypeStruct((pair_total, 2, pb_count, width, share), BF16),
        in_specs=[smem, smem, hbm, hbm],
        out_specs=hbm,
        scratch_shapes=[
            pltpu.VMEM(orbitals.shape, BF16),
            pltpu.VMEM((row_devices, k_total, width, piece), BF16),
            pltpu.VMEM((row_count, point_total), BF16),
            pltpu.VMEM((point_total, row_count), BF16),
            pltpu.VMEM((pair_total, pb_count, 2 * width, piece), BF16),
            pltpu.VMEM((pair_total, row_devices, pb_count, 2 * width, piece), BF16),
            pltpu.VMEM((row_count, width), BF16),
            pltpu.VMEM((width, row_count), BF16),
            pltpu.VMEM((width, row_count), BF16),
            pltpu.VMEM((row_devices, row_count, width), BF16),
            pltpu.VMEM((pair_total, 2, width, row_count), F32),
            pltpu.VMEM((pair_total, 2, width, row_count), F32),
            pltpu.VMEM((pair_total, width, row_count), F32),
            pltpu.VMEM((pair_total, width, row_count), BF16),
            pltpu.VMEM((pair_total, width, row_count), BF16),
            pltpu.VMEM((pair_total, 2, pb_count, width, share), BF16),
            sems,
            sems,
            sems((pair_total, pb_count)),
            sems((pair_total, pb_count)),
            sems((pair_total, 3)),
            sems((pair_total, 3)),
            sems((pair_total, 3)),
            sems((pair_total, 3)),
            sems((pair_total, 3)),
            sems((pair_total, 3)),
            sems((pair_total, 2)),
            sems((pair_total, 2)),
            sems((pair_total,)),
            sems((pair_total,)),
            sems((pair_total, 2, pb_count)),
            sems((pair_total, 2, pb_count)),
        ],
        compiler_params=pltpu.CompilerParams(
            collective_id=1, has_side_effects=True, vmem_limit_bytes=60 * 1024 * 1024
        ),
    )(pairs, k_slot, orbitals, kernels)
    return pl.pallas_call(
        swift_combine,
        out_shape=jax.ShapeDtypeStruct((1, share, k_total * width), F32),
        in_specs=[smem, smem, vmem],
        out_specs=vmem,
        scratch_shapes=[pltpu.VMEM((k_total, width, share), F32)],
    )(pairs, pair_count, got)


def shards(kernels, orbitals, pairs, k_slot, pair_count):
    pb_count, row_devices = lax.axis_size("pb"), lax.axis_size("row")
    piece = orbitals.shape[0] // row_devices
    share = kernels.shape[1] // pb_count
    width = orbitals.shape[1] // k_slot.shape[0]
    whole_tiles = piece % 128 == 0 and share % 128 == 0 and width % 16 == 0
    paired = row_devices == 4 and pb_count % row_devices == 0 and pb_count >= 8
    form = swift_shards if whole_tiles and paired else plain_shards
    return form(kernels, orbitals, pairs, k_slot, pair_count)


def solution(mesh):
    placed = (P("pb", "row", None), P("pb", None), P(), P(), P())
    return jax.shard_map(
        shards, mesh=mesh, in_specs=placed, out_specs=P("row", "pb", None), check_vma=False
    )
```

```python
import functools

import jax
import jax.numpy as jnp
from jax import lax
from jax.experimental import pallas as pl
from jax.experimental.pallas import tpu as pltpu
from jax.sharding import PartitionSpec as P

MESH = pl.DeviceIdType.MESH
BF16 = jnp.bfloat16
F32 = jnp.float32
NT = (((1,), (1,)), ((), ()))


def pick_kernel(width, pairs_ref, slot_ref, orb_ref, out_ref):
    pair_total, pb_count, piece, lanes = out_ref.shape
    rows = pl.ds(pl.multiple_of(lax.axis_index("row") * piece, piece), piece)
    low = lax.broadcasted_iota(jnp.int32, (piece, lanes), 1) < width

    def fetch(k, want):
        slot = slot_ref[k]
        block = orb_ref[rows, pl.ds(pl.multiple_of((slot >> 1) * lanes, lanes), lanes)].astype(F32)
        moved = pltpu.roll(block, width, 1)
        return jnp.where((slot & 1) == want, block, moved)

    def step(q, carry):
        for p in range(pair_total):
            left = fetch(pairs_ref[q, p, 0], 0)
            right = fetch(pairs_ref[q, p, 1], 1)
            out_ref[p, q] = jnp.where(low, left, right).astype(BF16)
        return carry

    lax.fori_loop(0, pb_count, step, 0)


def main_kernel(dims, picked, kern, out, w, basis, rows_r, rows_l, rows_t, f1, f2s, f2r, cbuf,
                w_sem, d_send, d_recv, g_send, g_recv, h_send, h_recv, y_send, y_recv,
                s_send, s_recv, c_send, c_recv):
    pb_count, row_devices, pair_total, piece, width = dims
    pb, row = lax.axis_index("pb"), lax.axis_index("row")
    chips = row_devices // 2
    part, chip = lax.rem(row, 2), lax.div(row, 2)
    mate = row + 1 - 2 * part
    row_count = w.shape[0]
    lanes = basis.shape[4]
    share = row_count // pb_count
    order = [(e, flip) for e in range(1, chips) for flip in (0, 1)] + [(0, 1), (0, 0)]

    def peer(e, flip):
        side = 1 - part if flip else part
        return 2 * lax.rem(chip + e, chips) + side

    w_copy = pltpu.make_async_copy(kern.at[0], w, w_sem)
    w_copy.start()

    barrier = pltpu.get_barrier_semaphore()

    def greet_pb(d, c):
        pl.semaphore_signal(barrier, inc=1, device_id=(lax.rem(pb + d, pb_count), row), device_id_type=MESH)
        return c

    def greet_row(d, c):
        pl.semaphore_signal(barrier, inc=1, device_id=(pb, lax.rem(row + d, row_devices)), device_id_type=MESH)
        return c

    lax.fori_loop(1, pb_count, greet_pb, 0)
    lax.fori_loop(1, row_devices, greet_row, 0)
    pl.semaphore_wait(barrier, pb_count + row_devices - 2)

    def spot(p, j, which):
        return basis.at[p, j, which]

    def points(p, r):
        span = pb_count // row_devices
        return basis[p, pl.ds(r * span, span)].reshape(row_count, lanes)

    def own(p):
        return pltpu.make_async_copy(picked.at[p, pb], spot(p, pb, row), d_recv.at[p, 0])

    def direct(p, d):
        q = lax.rem(pb + d, pb_count)
        return pltpu.make_async_remote_copy(
            src_ref=picked.at[p, q], dst_ref=spot(p, pb, row),
            send_sem=d_send.at[p, d], recv_sem=d_recv.at[p, d],
            device_id=(q, row), device_id_type=MESH)

    def across(p, e):
        block = basis.at[p, :, row]
        return pltpu.make_async_remote_copy(
            src_ref=block, dst_ref=block, send_sem=y_send.at[p, e - 1], recv_sem=y_recv.at[p, e - 1],
            device_id=(pb, peer(e, 0)), device_id_type=MESH)

    def to_mate(p):
        block = basis.at[p, :, row]
        return pltpu.make_async_remote_copy(
            src_ref=block, dst_ref=block, send_sem=g_send.at[p], recv_sem=g_recv.at[p],
            device_id=(pb, mate), device_id_type=MESH)

    def onward(p, e):
        block = basis.at[p, :, peer(chips - e, 0)]
        return pltpu.make_async_remote_copy(
            src_ref=block, dst_ref=block, send_sem=h_send.at[p, e - 1], recv_sem=h_recv.at[p, e - 1],
            device_id=(pb, mate), device_id_type=MESH)

    def shed(p, s):
        to = peer(*order[s])
        return pltpu.make_async_remote_copy(
            src_ref=f2s.at[p, s], dst_ref=f2r.at[p, s], send_sem=s_send.at[p, s], recv_sem=s_recv.at[p, s],
            device_id=(pb, to), device_id_type=MESH)

    def c_rows(j):
        return pl.ds(pl.multiple_of(j * share, share), share)

    def own_c(p):
        return pltpu.make_async_copy(cbuf.at[p, c_rows(pb)], out.at[p, pb], c_recv.at[p, 0])

    def give(p, d):
        j = lax.rem(pb + d, pb_count)
        return pltpu.make_async_remote_copy(
            src_ref=cbuf.at[p, c_rows(j)], dst_ref=out.at[p, pb], send_sem=c_send.at[p, d], recv_sem=c_recv.at[p, d],
            device_id=(j, row), device_id_type=MESH)

    def loop(low, high, body):
        def step(i, c):
            body(i)
            return c
        lax.fori_loop(low, high, step, 0)

    def send_pair(p):
        own(p).start()
        loop(1, pb_count, lambda d: direct(p, d).start())

    loop(0, pair_total, send_pair)

    def spread(p):
        own(p).wait()
        loop(1, pb_count, lambda d: direct(p, d).wait_recv())
        for e in range(1, chips):
            across(p, e).start()
        to_mate(p).start()

    def pass_far(p):
        for e in range(1, chips):
            across(p, e).wait_recv()
            onward(p, e).start()

    low = lax.broadcasted_iota(jnp.int32, (row_count, lanes), 1) < width

    def finish_pair(p):
        total = f2s[p, row_devices - 1].astype(F32)
        for s in range(row_devices - 1):
            shed(p, s).wait_recv()
            total = total + f2r[p, s].astype(F32)
        stacked = jnp.concatenate([jnp.zeros_like(total), total], axis=0)
        cbuf[p] = jnp.where(low, f1[p], stacked.T).astype(BF16)
        loop(1, pb_count, lambda d: give(p, d).start())
        own_c(p).start()

    def tile_of(p, s):
        to = peer(*order[s])
        cols = pl.ds(pl.multiple_of(to * row_count, row_count), row_count)
        there = points(p, to)
        second = None
        chunk = row_count // 2
        for m in range(2):
            here = slice(m * chunk, (m + 1) * chunk)
            weight = w[here, cols].astype(F32)
            gram = lax.dot_general(rows_r[here], there, NT, preferred_element_type=F32)
            first = jnp.dot((weight * gram).astype(BF16), there, preferred_element_type=F32)
            f1[p, here] = first if s == 0 else f1[p, here] + first
            gram = lax.dot_general(rows_l[here], there, NT, preferred_element_type=F32)
            term = jnp.dot(rows_t[:, here], (weight * gram).astype(BF16), preferred_element_type=F32)
            second = term if second is None else second + term
        f2s[p, s] = second[width:].astype(BF16)
        if s < row_devices - 1:
            shed(p, s).start()

    spread(0)
    pass_far(0)
    w_copy.wait()

    def pair_step(p):
        to_mate(p).wait_recv()
        for e in range(1, chips):
            onward(p, e).wait_recv()
        mine = points(p, row).astype(F32)
        rows_r[...] = jnp.where(low, 0, mine).astype(BF16)
        rows_l[...] = jnp.where(low, mine, 0).astype(BF16)
        rows_t[...] = mine.T.astype(BF16)
        for s in range(row_devices):
            tile_of(p, s)
            if s == 0:
                pl.when(p + 1 < pair_total)(lambda: spread(p + 1))
                pl.when(p > 0)(lambda: finish_pair(p - 1))
            if s == row_devices - 2:
                pl.when(p + 1 < pair_total)(lambda: pass_far(p + 1))

    loop(0, pair_total, pair_step)
    finish_pair(pair_total - 1)

    def settle(p):
        own_c(p).wait()

        to_mate(p).wait_send()
        for e in range(1, chips):
            across(p, e).wait_send()
            onward(p, e).wait_send()

        def one(d):
            direct(p, d).wait_send()
            give(p, d).wait()

        loop(1, pb_count, one)
        for s in range(row_devices - 1):
            shed(p, s).wait_send()

    loop(0, pair_total, settle)


def combine_kernel(width, pairs_ref, count_ref, got_ref, out_ref):
    pair_total, pb_count, share, lanes = got_ref.shape
    low = lax.broadcasted_iota(jnp.int32, (share, lanes), 1) < width
    out_ref[...] = jnp.zeros_like(out_ref)

    def step(q, carry):
        for p in range(pair_total):
            live = p < count_ref[q]
            block = jnp.where(live, got_ref[p, q].astype(F32), 0.0)
            moved = pltpu.roll(block, width, 1)
            for side in range(2):
                k = pairs_ref[q, p, side]
                odd = k & 1
                value = jnp.where(odd == side, block, moved)
                value = jnp.where(low == (odd == 0), value, 0.0)
                spot = pl.ds(pl.multiple_of((k >> 1) * lanes, lanes), lanes)
                out_ref[0, :, spot] += value
        return carry

    lax.fori_loop(0, pb_count, step, 0)


def plain_shards(kernels, orbitals, pairs, k_slot, pair_count):
    pb_count, row_devices = lax.axis_size("pb"), lax.axis_size("row")
    row_count, point_total = kernels.shape[1:]
    pair_total = pairs.shape[1]
    k_total = k_slot.shape[0]
    width = orbitals.shape[1] // k_total
    lanes = 2 * width
    piece = orbitals.shape[0] // row_devices
    far = max(row_devices // 2 - 1, 1)
    share = row_count // pb_count
    smem = pl.BlockSpec(memory_space=pltpu.SMEM)
    vmem = pl.BlockSpec(memory_space=pltpu.VMEM)
    hbm = pl.BlockSpec(memory_space=pl.ANY)
    picked = pl.pallas_call(
        functools.partial(pick_kernel, width),
        out_shape=jax.ShapeDtypeStruct((pair_total, pb_count, piece, lanes), BF16),
        in_specs=[smem, smem, vmem],
        out_specs=vmem,
    )(pairs, k_slot, orbitals)
    sems = pltpu.SemaphoreType.DMA
    got = pl.pallas_call(
        functools.partial(main_kernel, (pb_count, row_devices, pair_total, piece, width)),
        out_shape=jax.ShapeDtypeStruct((pair_total, pb_count, share, lanes), BF16),
        in_specs=[hbm, hbm],
        out_specs=hbm,
        scratch_shapes=[
            pltpu.VMEM((row_count, point_total), BF16),
            pltpu.VMEM((pair_total, pb_count, row_devices, piece, lanes), BF16),
            pltpu.VMEM((row_count, lanes), BF16),
            pltpu.VMEM((row_count, lanes), BF16),
            pltpu.VMEM((lanes, row_count), BF16),
            pltpu.VMEM((pair_total, row_count, lanes), F32),
            pltpu.VMEM((pair_total, row_devices, width, row_count), BF16),
            pltpu.VMEM((pair_total, row_devices, width, row_count), BF16),
            pltpu.VMEM((pair_total, row_count, lanes), BF16),
            sems,
            sems((pair_total, pb_count)),
            sems((pair_total, pb_count)),
            sems((pair_total,)),
            sems((pair_total,)),
            sems((pair_total, far)),
            sems((pair_total, far)),
            sems((pair_total, far)),
            sems((pair_total, far)),
            sems((pair_total, row_devices)),
            sems((pair_total, row_devices)),
            sems((pair_total, pb_count)),
            sems((pair_total, pb_count)),
        ],
        compiler_params=pltpu.CompilerParams(
            collective_id=0, has_side_effects=True, vmem_limit_bytes=56 * 1024 * 1024
        ),
    )(picked, kernels)
    return pl.pallas_call(
        functools.partial(combine_kernel, width),
        out_shape=jax.ShapeDtypeStruct((1, share, k_total * width), F32),
        in_specs=[smem, smem, vmem],
        out_specs=vmem,
    )(pairs, pair_count, got)


def swift_kernel(dims, pairs_ref, slot_ref, orb, kern, out, orb_v, orb_t, w, wt, picked, basis, rows_l, rows_r,
                 rows_p, nat_r, l1s, l1r, keep, l2s, l2r, cbuf, o_sem, w_sem, d_send, d_recv, x_send, x_recv,
                 g_send, g_recv, h_send, h_recv, a_send, a_recv, b_send, b_recv, c_send, c_recv, own_sem):
    pb_count, pair_total, piece, width = dims
    pb, row = lax.axis_index("pb"), lax.axis_index("row")
    row_devices = basis.shape[1]
    row_count, point_total = w.shape
    span = pb_count // row_devices
    half = pb_count // 2
    share = row_count // pb_count
    part, chip = lax.rem(row, 2), lax.div(row, 2)
    side_x, side_z = lax.rem(pb, 2), lax.div(pb, 2)
    mate = row + 1 - 2 * part
    far = 2 * (1 - chip) + part
    bounds = [1, half, half + half // 2, pb_count]
    groups = range(3)
    group_of = [0] + [g for g in groups for m in range(bounds[g], bounds[g + 1])]

    turned = [side_x, 1 - side_x]
    ahead = [lax.rem(side_z + m // 2, half) * 2 + turned[m % 2] for m in range(pb_count)]

    def slots_of(s):
        picks = []
        for i in range(span):
            j = s * span + i
            dz = lax.rem(side_z - lax.div(j, 2) + half, half)
            picks.append(2 * dz + lax.rem(side_x + j, 2))
        return picks

    slots = [slots_of(jnp.int32(s)) for s in range(row_devices)]
    diagonal = 2 * (1 - chip) + 1 - part
    order = [diagonal, far, mate, row]
    order_slots = [slots_of(s) for s in order]
    others = range(1, pb_count)

    def loop(low, high, body):
        def step(i, c):
            body(i)
            return c
        lax.fori_loop(low, high, step, 0)

    orb_copy = pltpu.make_async_copy(orb, orb_v, o_sem)
    orb_copy.start()
    w_copy = pltpu.make_async_copy(kern.at[0], w, w_sem)
    w_copy.start()

    barrier = pltpu.get_barrier_semaphore()
    loop(1, pb_count, lambda m: pl.semaphore_signal(
        barrier, inc=1, device_id=(lax.rem(pb + m, pb_count), row), device_id_type=MESH))
    pl.semaphore_signal(barrier, inc=1, device_id=(pb, mate), device_id_type=MESH)
    pl.semaphore_signal(barrier, inc=1, device_id=(pb, far), device_id_type=MESH)

    def direct(p, m):
        return pltpu.make_async_remote_copy(
            src_ref=picked.at[p, m], dst_ref=basis.at[p, row, m],
            send_sem=d_send, recv_sem=d_recv.at[p, group_of[m]],
            device_id=(ahead[m], row), device_id_type=MESH)

    def passed(p, g, quarter, to, send, recv):
        block = basis.at[p, quarter, pl.ds(bounds[g], bounds[g + 1] - bounds[g])]
        return pltpu.make_async_remote_copy(
            src_ref=block, dst_ref=block, send_sem=send, recv_sem=recv.at[p, g],
            device_id=(pb, to), device_id_type=MESH)

    def across(p, g):
        return passed(p, g, row, far, x_send, x_recv)

    def to_mate(p, g):
        return passed(p, g, row, mate, g_send, g_recv)

    def onward(p, g):
        return passed(p, g, far, mate, h_send, h_recv)

    def fold(p, i):
        return pltpu.make_async_remote_copy(
            src_ref=l1s.at[p, i], dst_ref=l1r.at[p, i], send_sem=a_send, recv_sem=a_recv.at[p, i],
            device_id=(pb, mate), device_id_type=MESH)

    def shed(p):
        return pltpu.make_async_remote_copy(
            src_ref=l2s.at[p], dst_ref=l2r.at[p], send_sem=b_send, recv_sem=b_recv.at[p],
            device_id=(pb, far), device_id_type=MESH)

    def give(p, side, m):
        return pltpu.make_async_remote_copy(
            src_ref=cbuf.at[p, side, ahead[m]], dst_ref=out.at[p, side, pb],
            send_sem=c_send, recv_sem=c_recv, device_id=(ahead[m], row), device_id_type=MESH)

    def own_c(p, side):
        return pltpu.make_async_copy(cbuf.at[p, side, pb], out.at[p, side, pb], own_sem)

    def take(quarter, k):
        return orb_t[quarter, slot_ref[k]]

    orb_copy.wait()

    def turn(r):
        block = orb_v[pl.ds(pl.multiple_of(r * piece, piece), piece), :].T
        orb_t[r] = block.reshape(orb_t.shape[1:])

    turn(row)

    def pick(p):
        for m in others:
            for side in range(2):
                picked[p, m, side * width:(side + 1) * width] = take(row, pairs_ref[p, side, ahead[m]])

    def send(p):
        for m in others:
            direct(p, m).start()

    pick(0)
    pl.semaphore_wait(barrier, pb_count + 1)
    send(0)

    loop(1, pair_total, pick)
    loop(1, row_devices, lambda e: turn(lax.rem(row + e, row_devices)))

    def own(p):
        def one(r):
            for side in range(2):
                basis[p, r, 0, side * width:(side + 1) * width] = take(r, pairs_ref[p, side, pb])
        loop(0, row_devices, one)

    loop(0, pair_total, own)

    def spread(p, *which):
        for g in which:
            arrived = basis.at[p, row, pl.ds(bounds[g], bounds[g + 1] - bounds[g])]
            pltpu.make_async_copy(arrived, arrived, d_recv.at[p, g]).wait()
            across(p, g).start()
            to_mate(p, g).start()

    def pass_far(p, *which):
        for g in which:
            across(p, g).wait_recv()
            onward(p, g).start()

    def turn_w(i):
        cols = pl.ds(pl.multiple_of(i * row_count // 2, row_count // 2), row_count // 2)
        for b in range(pb_count):
            at = (b % 2) * half + b // 2
            wt[cols, at * share:(at + 1) * share] = w[b * share:(b + 1) * share, cols].T

    w_copy.wait()
    steps = point_total * 2 // row_count
    turn_w(0)
    spread(0, 0)
    loop(1, steps // 2, turn_w)
    spread(0, 1)
    send(1)
    turn_w(steps // 2)
    spread(0, 2)
    loop(steps // 2 + 1, steps - 2, turn_w)
    pass_far(0, 0)
    send(2)
    loop(steps - 2, steps, turn_w)
    pass_far(0, 1)
    loop(3, pair_total, send)
    pass_far(0, 2)

    def tile_t(p, at, side):
        lanes = slice(side * width, (side + 1) * width)
        return jnp.concatenate([basis[p, r, m, lanes, :] for m in at for r in range(row_devices)], axis=1)

    def finish(p):
        fold(p, 1).wait_recv()
        shed(p).wait_recv()
        total = keep[p, 1] + l1r[p, 1] + l2r[p].astype(F32)
        for j in range(pb_count):
            cbuf[p, 1, j] = total[:, j * share:(j + 1) * share].astype(BF16)
        for m in others:
            give(p, 1, m).start()
        own_c(p, 1).start()

    def column_tile(p, n):
        s = order[n]
        cols = pl.ds(pl.multiple_of(s * row_count, row_count), row_count)
        there_l, there_r = tile_t(p, order_slots[n], 0), tile_t(p, order_slots[n], 1)
        nat_r[s] = there_r.T
        total = None
        chunk = row_count // 2
        for m in range(2):
            here = slice(m * chunk, (m + 1) * chunk)
            gram = jnp.dot(rows_l[here], there_l, preferred_element_type=F32)
            term = jnp.dot(rows_r[:, here], (w[here, cols].astype(F32) * gram).astype(BF16), preferred_element_type=F32)
            total = term if total is None else total + term
        return total

    def row_tile(p, h, s):
        lanes = slice(h * row_count // 2, (h + 1) * row_count // 2)
        gram = jnp.dot(nat_r[s], rows_p[:, lanes], preferred_element_type=F32)
        rows = slice(s * row_count, (s + 1) * row_count)
        return jnp.dot(tile_t(p, slots[s], 0), (wt[rows, lanes].astype(F32) * gram).astype(BF16), preferred_element_type=F32)

    def row_half(p, h):
        total = None
        for s in range(row_devices):
            term = row_tile(p, h, s)
            total = term if total is None else total + term
        for i in range(half):
            cbuf[p, 0, 2 * i + h] = total[:, i * share:(i + 1) * share].astype(BF16)

        def send_same():
            own_c(p, 0).start()
            for m in range(2, pb_count, 2):
                give(p, 0, m).start()

        def send_turned():
            for m in range(1, pb_count, 2):
                give(p, 0, m).start()

        pl.when(side_x == h)(send_same)
        pl.when(side_x != h)(send_turned)

    def pair_step(p):
        more, more_later = p + 1 < pair_total, p + 2 < pair_total
        for g in groups:
            to_mate(p, g).wait_recv()
            onward(p, g).wait_recv()

        pl.when(p == 0)(lambda: spread(p + 1, 0, 1))
        rows_l[...] = tile_t(p, order_slots[3], 0).T
        right = tile_t(p, order_slots[3], 1)
        rows_r[...] = right
        spun = [b for h in range(2) for b in range(h, pb_count, 2)]
        rows_p[...] = jnp.concatenate([right[:, b * share:(b + 1) * share] for b in spun], axis=1)

        l1s[p, 0] = column_tile(p, 0)
        keep[p, 0] = column_tile(p, 1)
        fold(p, 0).start()

        pl.when(p == 0)(lambda: spread(p + 1, 2))
        pl.when((p == 1) & more)(lambda: spread(p + 1, 1, 2))
        pl.when(p > 0)(lambda: finish(p - 1))

        l1s[p, 1] = column_tile(p, 2)
        keep[p, 1] = column_tile(p, 3)
        fold(p, 1).start()
        fold(p, 0).wait_recv()
        l2s[p] = (keep[p, 0] + l1r[p, 0]).astype(BF16)
        shed(p).start()

        pl.when((p > 1) & more)(lambda: pass_far(p + 1, 0))
        row_half(p, 0)
        pl.when((p < 2) & more)(lambda: pass_far(p + 1, 0))
        pl.when((p > 1) & more)(lambda: pass_far(p + 1, 1, 2))
        row_half(p, 1)
        pl.when((p == 0) & more_later)(lambda: spread(p + 2, 0))
        pl.when((p > 0) & more_later)(lambda: spread(p + 2, 0, 1, 2))
        pl.when((p < 2) & more)(lambda: pass_far(p + 1, 1, 2))

    loop(0, pair_total, pair_step)
    finish(pair_total - 1)

    def sent(ref, sem):
        pltpu.make_async_copy(ref, ref, sem).wait()

    for sem in (x_send, g_send, h_send):
        sent(basis.at[:, 0, pl.ds(1, pb_count - 1)], sem)
    sent(picked.at[:, pl.ds(1, pb_count - 1)], d_send)
    sent(l1s, a_send)
    sent(l2s, b_send)
    sent(cbuf.at[:, :, pl.ds(1, pb_count - 1)], c_send)
    sent(cbuf.at[:, :, 0], own_sem)
    arrived = out.at[:, :, pl.ds(1, pb_count - 1)]
    sent(arrived, c_recv)


def swift_combine(pairs_ref, count_ref, got_ref, out_ref, total):
    pair_total, sides, pb_count, width, share = got_ref.shape
    total[...] = jnp.zeros_like(total)

    def step(q, carry):
        for p in range(pair_total):
            live = p < count_ref[q]
            for side in range(sides):
                k = pairs_ref[p, side, q]
                total[k] += jnp.where(live, got_ref[p, side, q].astype(F32), 0.0)
        return carry

    lax.fori_loop(0, pb_count, step, 0)
    out_ref[0] = total[...].reshape(total.shape[0] * width, share).T


def swift_shards(kernels, orbitals, pairs, k_slot, pair_count):
    pb_count, row_devices = lax.axis_size("pb"), lax.axis_size("row")
    row_count, point_total = kernels.shape[1:]
    pair_total = pairs.shape[1]
    k_total = k_slot.shape[0]
    width = orbitals.shape[1] // k_total
    piece = orbitals.shape[0] // row_devices
    share = row_count // pb_count
    pairs = jnp.transpose(pairs, (1, 2, 0))
    smem = pl.BlockSpec(memory_space=pltpu.SMEM)
    vmem = pl.BlockSpec(memory_space=pltpu.VMEM)
    hbm = pl.BlockSpec(memory_space=pl.ANY)
    sems = pltpu.SemaphoreType.DMA
    got = pl.pallas_call(
        functools.partial(swift_kernel, (pb_count, pair_total, piece, width)),
        out_shape=jax.ShapeDtypeStruct((pair_total, 2, pb_count, width, share), BF16),
        in_specs=[smem, smem, hbm, hbm],
        out_specs=hbm,
        scratch_shapes=[
            pltpu.VMEM(orbitals.shape, BF16),
            pltpu.VMEM((row_devices, k_total, width, piece), BF16),
            pltpu.VMEM((row_count, point_total), BF16),
            pltpu.VMEM((point_total, row_count), BF16),
            pltpu.VMEM((pair_total, pb_count, 2 * width, piece), BF16),
            pltpu.VMEM((pair_total, row_devices, pb_count, 2 * width, piece), BF16),
            pltpu.VMEM((row_count, width), BF16),
            pltpu.VMEM((width, row_count), BF16),
            pltpu.VMEM((width, row_count), BF16),
            pltpu.VMEM((row_devices, row_count, width), BF16),
            pltpu.VMEM((pair_total, 2, width, row_count), F32),
            pltpu.VMEM((pair_total, 2, width, row_count), F32),
            pltpu.VMEM((pair_total, 2, width, row_count), F32),
            pltpu.VMEM((pair_total, width, row_count), BF16),
            pltpu.VMEM((pair_total, width, row_count), BF16),
            pltpu.VMEM((pair_total, 2, pb_count, width, share), BF16),
            sems,
            sems,
            sems,
            sems((pair_total, 3)),
            sems,
            sems((pair_total, 3)),
            sems,
            sems((pair_total, 3)),
            sems,
            sems((pair_total, 3)),
            sems,
            sems((pair_total, 2)),
            sems,
            sems((pair_total,)),
            sems,
            sems,
            sems,
        ],
        compiler_params=pltpu.CompilerParams(
            collective_id=1, has_side_effects=True, vmem_limit_bytes=60 * 1024 * 1024
        ),
    )(pairs, k_slot, orbitals, kernels)
    return pl.pallas_call(
        swift_combine,
        out_shape=jax.ShapeDtypeStruct((1, share, k_total * width), F32),
        in_specs=[smem, smem, vmem],
        out_specs=vmem,
        scratch_shapes=[pltpu.VMEM((k_total, width, share), F32)],
    )(pairs, pair_count, got)


def shards(kernels, orbitals, pairs, k_slot, pair_count):
    pb_count, row_devices = lax.axis_size("pb"), lax.axis_size("row")
    piece = orbitals.shape[0] // row_devices
    share = kernels.shape[1] // pb_count
    width = orbitals.shape[1] // k_slot.shape[0]
    whole_tiles = piece % 128 == 0 and share % 128 == 0 and width % 16 == 0
    paired = row_devices == 4 and pb_count % row_devices == 0 and pb_count >= 8 and pairs.shape[1] > 2
    form = swift_shards if whole_tiles and paired else plain_shards
    return form(kernels, orbitals, pairs, k_slot, pair_count)


def solution(mesh):
    placed = (P("pb", "row", None), P("pb", None), P(), P(), P())
    return jax.shard_map(
        shards, mesh=mesh, in_specs=placed, out_specs=P("row", "pb", None), check_vma=False
    )
```

```python
import functools

import jax
import jax.numpy as jnp
from jax import lax
from jax.experimental import pallas as pl
from jax.experimental.pallas import tpu as pltpu
from jax.sharding import PartitionSpec as P

MESH = pl.DeviceIdType.MESH
BF16 = jnp.bfloat16
F32 = jnp.float32
NT = (((1,), (1,)), ((), ()))


def pick_kernel(width, pairs_ref, slot_ref, orb_ref, out_ref):
    pair_total, pb_count, piece, lanes = out_ref.shape
    rows = pl.ds(pl.multiple_of(lax.axis_index("row") * piece, piece), piece)
    low = lax.broadcasted_iota(jnp.int32, (piece, lanes), 1) < width

    def fetch(k, want):
        slot = slot_ref[k]
        block = orb_ref[rows, pl.ds(pl.multiple_of((slot >> 1) * lanes, lanes), lanes)].astype(F32)
        moved = pltpu.roll(block, width, 1)
        return jnp.where((slot & 1) == want, block, moved)

    def step(q, carry):
        for p in range(pair_total):
            left = fetch(pairs_ref[q, p, 0], 0)
            right = fetch(pairs_ref[q, p, 1], 1)
            out_ref[p, q] = jnp.where(low, left, right).astype(BF16)
        return carry

    lax.fori_loop(0, pb_count, step, 0)


def main_kernel(dims, picked, kern, out, w, basis, rows_r, rows_l, rows_t, f1, f2s, f2r, cbuf,
                w_sem, d_send, d_recv, g_send, g_recv, h_send, h_recv, y_send, y_recv,
                s_send, s_recv, c_send, c_recv):
    pb_count, row_devices, pair_total, piece, width = dims
    pb, row = lax.axis_index("pb"), lax.axis_index("row")
    chips = row_devices // 2
    part, chip = lax.rem(row, 2), lax.div(row, 2)
    mate = row + 1 - 2 * part
    row_count = w.shape[0]
    lanes = basis.shape[4]
    share = row_count // pb_count
    order = [(e, flip) for e in range(1, chips) for flip in (0, 1)] + [(0, 1), (0, 0)]

    def peer(e, flip):
        side = 1 - part if flip else part
        return 2 * lax.rem(chip + e, chips) + side

    w_copy = pltpu.make_async_copy(kern.at[0], w, w_sem)
    w_copy.start()

    barrier = pltpu.get_barrier_semaphore()

    def greet_pb(d, c):
        pl.semaphore_signal(barrier, inc=1, device_id=(lax.rem(pb + d, pb_count), row), device_id_type=MESH)
        return c

    def greet_row(d, c):
        pl.semaphore_signal(barrier, inc=1, device_id=(pb, lax.rem(row + d, row_devices)), device_id_type=MESH)
        return c

    lax.fori_loop(1, pb_count, greet_pb, 0)
    lax.fori_loop(1, row_devices, greet_row, 0)
    pl.semaphore_wait(barrier, pb_count + row_devices - 2)

    def spot(p, j, which):
        return basis.at[p, j, which]

    def points(p, r):
        span = pb_count // row_devices
        return basis[p, pl.ds(r * span, span)].reshape(row_count, lanes)

    def own(p):
        return pltpu.make_async_copy(picked.at[p, pb], spot(p, pb, row), d_recv.at[p, 0])

    def direct(p, d):
        q = lax.rem(pb + d, pb_count)
        return pltpu.make_async_remote_copy(
            src_ref=picked.at[p, q], dst_ref=spot(p, pb, row),
            send_sem=d_send.at[p, d], recv_sem=d_recv.at[p, d],
            device_id=(q, row), device_id_type=MESH)

    def across(p, e):
        block = basis.at[p, :, row]
        return pltpu.make_async_remote_copy(
            src_ref=block, dst_ref=block, send_sem=y_send.at[p, e - 1], recv_sem=y_recv.at[p, e - 1],
            device_id=(pb, peer(e, 0)), device_id_type=MESH)

    def to_mate(p):
        block = basis.at[p, :, row]
        return pltpu.make_async_remote_copy(
            src_ref=block, dst_ref=block, send_sem=g_send.at[p], recv_sem=g_recv.at[p],
            device_id=(pb, mate), device_id_type=MESH)

    def onward(p, e):
        block = basis.at[p, :, peer(chips - e, 0)]
        return pltpu.make_async_remote_copy(
            src_ref=block, dst_ref=block, send_sem=h_send.at[p, e - 1], recv_sem=h_recv.at[p, e - 1],
            device_id=(pb, mate), device_id_type=MESH)

    def shed(p, s):
        to = peer(*order[s])
        return pltpu.make_async_remote_copy(
            src_ref=f2s.at[p, s], dst_ref=f2r.at[p, s], send_sem=s_send.at[p, s], recv_sem=s_recv.at[p, s],
            device_id=(pb, to), device_id_type=MESH)

    def c_rows(j):
        return pl.ds(pl.multiple_of(j * share, share), share)

    def own_c(p):
        return pltpu.make_async_copy(cbuf.at[p, c_rows(pb)], out.at[p, pb], c_recv.at[p, 0])

    def give(p, d):
        j = lax.rem(pb + d, pb_count)
        return pltpu.make_async_remote_copy(
            src_ref=cbuf.at[p, c_rows(j)], dst_ref=out.at[p, pb], send_sem=c_send.at[p, d], recv_sem=c_recv.at[p, d],
            device_id=(j, row), device_id_type=MESH)

    def loop(low, high, body):
        def step(i, c):
            body(i)
            return c
        lax.fori_loop(low, high, step, 0)

    def send_pair(p):
        own(p).start()
        loop(1, pb_count, lambda d: direct(p, d).start())

    loop(0, pair_total, send_pair)

    def spread(p):
        own(p).wait()
        loop(1, pb_count, lambda d: direct(p, d).wait_recv())
        for e in range(1, chips):
            across(p, e).start()
        to_mate(p).start()

    def pass_far(p):
        for e in range(1, chips):
            across(p, e).wait_recv()
            onward(p, e).start()

    low = lax.broadcasted_iota(jnp.int32, (row_count, lanes), 1) < width

    def finish_pair(p):
        total = f2s[p, row_devices - 1].astype(F32)
        for s in range(row_devices - 1):
            shed(p, s).wait_recv()
            total = total + f2r[p, s].astype(F32)
        stacked = jnp.concatenate([jnp.zeros_like(total), total], axis=0)
        cbuf[p] = jnp.where(low, f1[p], stacked.T).astype(BF16)
        loop(1, pb_count, lambda d: give(p, d).start())
        own_c(p).start()

    def tile_of(p, s):
        to = peer(*order[s])
        cols = pl.ds(pl.multiple_of(to * row_count, row_count), row_count)
        there = points(p, to)
        second = None
        chunk = row_count // 2
        for m in range(2):
            here = slice(m * chunk, (m + 1) * chunk)
            weight = w[here, cols].astype(F32)
            gram = lax.dot_general(rows_r[here], there, NT, preferred_element_type=F32)
            first = jnp.dot((weight * gram).astype(BF16), there, preferred_element_type=F32)
            f1[p, here] = first if s == 0 else f1[p, here] + first
            gram = lax.dot_general(rows_l[here], there, NT, preferred_element_type=F32)
            term = jnp.dot(rows_t[:, here], (weight * gram).astype(BF16), preferred_element_type=F32)
            second = term if second is None else second + term
        f2s[p, s] = second[width:].astype(BF16)
        if s < row_devices - 1:
            shed(p, s).start()

    spread(0)
    pass_far(0)
    w_copy.wait()

    def pair_step(p):
        to_mate(p).wait_recv()
        for e in range(1, chips):
            onward(p, e).wait_recv()
        mine = points(p, row).astype(F32)
        rows_r[...] = jnp.where(low, 0, mine).astype(BF16)
        rows_l[...] = jnp.where(low, mine, 0).astype(BF16)
        rows_t[...] = mine.T.astype(BF16)
        for s in range(row_devices):
            tile_of(p, s)
            if s == 0:
                pl.when(p + 1 < pair_total)(lambda: spread(p + 1))
                pl.when(p > 0)(lambda: finish_pair(p - 1))
            if s == row_devices - 2:
                pl.when(p + 1 < pair_total)(lambda: pass_far(p + 1))

    loop(0, pair_total, pair_step)
    finish_pair(pair_total - 1)

    def settle(p):
        own_c(p).wait()

        to_mate(p).wait_send()
        for e in range(1, chips):
            across(p, e).wait_send()
            onward(p, e).wait_send()

        def one(d):
            direct(p, d).wait_send()
            give(p, d).wait()

        loop(1, pb_count, one)
        for s in range(row_devices - 1):
            shed(p, s).wait_send()

    loop(0, pair_total, settle)


def combine_kernel(width, pairs_ref, count_ref, got_ref, out_ref):
    pair_total, pb_count, share, lanes = got_ref.shape
    low = lax.broadcasted_iota(jnp.int32, (share, lanes), 1) < width
    out_ref[...] = jnp.zeros_like(out_ref)

    def step(q, carry):
        for p in range(pair_total):
            live = p < count_ref[q]
            block = jnp.where(live, got_ref[p, q].astype(F32), 0.0)
            moved = pltpu.roll(block, width, 1)
            for side in range(2):
                k = pairs_ref[q, p, side]
                odd = k & 1
                value = jnp.where(odd == side, block, moved)
                value = jnp.where(low == (odd == 0), value, 0.0)
                spot = pl.ds(pl.multiple_of((k >> 1) * lanes, lanes), lanes)
                out_ref[0, :, spot] += value
        return carry

    lax.fori_loop(0, pb_count, step, 0)


def plain_shards(kernels, orbitals, pairs, k_slot, pair_count):
    pb_count, row_devices = lax.axis_size("pb"), lax.axis_size("row")
    row_count, point_total = kernels.shape[1:]
    pair_total = pairs.shape[1]
    k_total = k_slot.shape[0]
    width = orbitals.shape[1] // k_total
    lanes = 2 * width
    piece = orbitals.shape[0] // row_devices
    far = max(row_devices // 2 - 1, 1)
    share = row_count // pb_count
    smem = pl.BlockSpec(memory_space=pltpu.SMEM)
    vmem = pl.BlockSpec(memory_space=pltpu.VMEM)
    hbm = pl.BlockSpec(memory_space=pl.ANY)
    picked = pl.pallas_call(
        functools.partial(pick_kernel, width),
        out_shape=jax.ShapeDtypeStruct((pair_total, pb_count, piece, lanes), BF16),
        in_specs=[smem, smem, vmem],
        out_specs=vmem,
    )(pairs, k_slot, orbitals)
    sems = pltpu.SemaphoreType.DMA
    got = pl.pallas_call(
        functools.partial(main_kernel, (pb_count, row_devices, pair_total, piece, width)),
        out_shape=jax.ShapeDtypeStruct((pair_total, pb_count, share, lanes), BF16),
        in_specs=[hbm, hbm],
        out_specs=hbm,
        scratch_shapes=[
            pltpu.VMEM((row_count, point_total), BF16),
            pltpu.VMEM((pair_total, pb_count, row_devices, piece, lanes), BF16),
            pltpu.VMEM((row_count, lanes), BF16),
            pltpu.VMEM((row_count, lanes), BF16),
            pltpu.VMEM((lanes, row_count), BF16),
            pltpu.VMEM((pair_total, row_count, lanes), F32),
            pltpu.VMEM((pair_total, row_devices, width, row_count), BF16),
            pltpu.VMEM((pair_total, row_devices, width, row_count), BF16),
            pltpu.VMEM((pair_total, row_count, lanes), BF16),
            sems,
            sems((pair_total, pb_count)),
            sems((pair_total, pb_count)),
            sems((pair_total,)),
            sems((pair_total,)),
            sems((pair_total, far)),
            sems((pair_total, far)),
            sems((pair_total, far)),
            sems((pair_total, far)),
            sems((pair_total, row_devices)),
            sems((pair_total, row_devices)),
            sems((pair_total, pb_count)),
            sems((pair_total, pb_count)),
        ],
        compiler_params=pltpu.CompilerParams(
            collective_id=0, has_side_effects=True, vmem_limit_bytes=56 * 1024 * 1024
        ),
    )(picked, kernels)
    return pl.pallas_call(
        functools.partial(combine_kernel, width),
        out_shape=jax.ShapeDtypeStruct((1, share, k_total * width), F32),
        in_specs=[smem, smem, vmem],
        out_specs=vmem,
    )(pairs, pair_count, got)


def swift_kernel(dims, pairs_ref, slot_ref, orb, kern, out, orb_v, orb_t, w, wt, picked, basis, rows_l, rows_r,
                 rows_p, nat_r, l1s, l1r, keep, l2s, l2r, cbuf, o_sem, w_sem, d_send, d_recv, x_send, x_recv,
                 g_send, g_recv, h_send, h_recv, a_send, a_recv, b_send, b_recv, c_send, c_recv, own_sem):
    pb_count, pair_total, piece, width = dims
    pb, row = lax.axis_index("pb"), lax.axis_index("row")
    row_devices = basis.shape[1]
    row_count, point_total = w.shape
    span = pb_count // row_devices
    half = pb_count // 2
    share = row_count // pb_count
    part, chip = lax.rem(row, 2), lax.div(row, 2)
    side_x, side_z = lax.rem(pb, 2), lax.div(pb, 2)
    mate = row + 1 - 2 * part
    far = 2 * (1 - chip) + part
    bounds = [1, half, half + half // 2, pb_count]
    groups = range(3)
    group_of = [0] + [g for g in groups for m in range(bounds[g], bounds[g + 1])]

    turned = [side_x, 1 - side_x]
    ahead = [lax.rem(side_z + m // 2, half) * 2 + turned[m % 2] for m in range(pb_count)]

    def slots_of(s):
        picks = []
        for i in range(span):
            j = s * span + i
            dz = lax.rem(side_z - lax.div(j, 2) + half, half)
            picks.append(2 * dz + lax.rem(side_x + j, 2))
        return picks

    slots = [slots_of(jnp.int32(s)) for s in range(row_devices)]
    diagonal = 2 * (1 - chip) + 1 - part
    order = [diagonal, far, mate, row]
    order_slots = [slots_of(s) for s in order]
    others = range(1, pb_count)

    def loop(low, high, body):
        def step(i, c):
            body(i)
            return c
        lax.fori_loop(low, high, step, 0)

    orb_copy = pltpu.make_async_copy(orb, orb_v, o_sem)
    orb_copy.start()
    w_copy = pltpu.make_async_copy(kern.at[0], w, w_sem)
    w_copy.start()

    barrier = pltpu.get_barrier_semaphore()
    loop(1, pb_count, lambda m: pl.semaphore_signal(
        barrier, inc=1, device_id=(lax.rem(pb + m, pb_count), row), device_id_type=MESH))
    pl.semaphore_signal(barrier, inc=1, device_id=(pb, mate), device_id_type=MESH)
    pl.semaphore_signal(barrier, inc=1, device_id=(pb, far), device_id_type=MESH)

    def direct(p, m):
        return pltpu.make_async_remote_copy(
            src_ref=picked.at[p, m], dst_ref=basis.at[p, row, m],
            send_sem=d_send, recv_sem=d_recv.at[p, group_of[m]],
            device_id=(ahead[m], row), device_id_type=MESH)

    def passed(p, g, quarter, to, send, recv):
        block = basis.at[p, quarter, pl.ds(bounds[g], bounds[g + 1] - bounds[g])]
        return pltpu.make_async_remote_copy(
            src_ref=block, dst_ref=block, send_sem=send, recv_sem=recv.at[p, g],
            device_id=(pb, to), device_id_type=MESH)

    def across(p, g):
        return passed(p, g, row, far, x_send, x_recv)

    def to_mate(p, g):
        return passed(p, g, row, mate, g_send, g_recv)

    def onward(p, g):
        return passed(p, g, far, mate, h_send, h_recv)

    def fold(p, i):
        return pltpu.make_async_remote_copy(
            src_ref=l1s.at[p, i], dst_ref=l1r.at[p, i], send_sem=a_send, recv_sem=a_recv.at[p, i],
            device_id=(pb, mate), device_id_type=MESH)

    def shed(p):
        return pltpu.make_async_remote_copy(
            src_ref=l2s.at[p], dst_ref=l2r.at[p], send_sem=b_send, recv_sem=b_recv.at[p],
            device_id=(pb, far), device_id_type=MESH)

    def give(p, side, dz, x):
        to = 2 * lax.rem(side_z + dz, half) + x
        return pltpu.make_async_remote_copy(
            src_ref=cbuf.at[p, side, to], dst_ref=out.at[p, side, pb],
            send_sem=c_send, recv_sem=c_recv, device_id=(to, row), device_id_type=MESH)

    def own_c(p, side):
        return pltpu.make_async_copy(cbuf.at[p, side, pb], out.at[p, side, pb], own_sem)

    def take(quarter, k):
        return orb_t[quarter, slot_ref[k]]

    orb_copy.wait()

    def turn(r):
        block = orb_v[pl.ds(pl.multiple_of(r * piece, piece), piece), :].T
        orb_t[r] = block.reshape(orb_t.shape[1:])

    turn(row)

    def pick(p):
        for m in others:
            for side in range(2):
                picked[p, m, side * width:(side + 1) * width] = take(row, pairs_ref[p, side, ahead[m]])

    def send(p):
        for m in others:
            direct(p, m).start()

    pick(0)
    pl.semaphore_wait(barrier, pb_count + 1)
    send(0)

    loop(1, pair_total, pick)
    loop(1, row_devices, lambda e: turn(lax.rem(row + e, row_devices)))

    def own(p):
        def one(r):
            for side in range(2):
                basis[p, r, 0, side * width:(side + 1) * width] = take(r, pairs_ref[p, side, pb])
        loop(0, row_devices, one)

    loop(0, pair_total, own)

    def spread(p, *which):
        for g in which:
            arrived = basis.at[p, row, pl.ds(bounds[g], bounds[g + 1] - bounds[g])]
            pltpu.make_async_copy(arrived, arrived, d_recv.at[p, g]).wait()
            across(p, g).start()
            to_mate(p, g).start()

    def pass_far(p, *which):
        for g in which:
            across(p, g).wait_recv()
            onward(p, g).start()

    def turn_w(i):
        cols = pl.ds(pl.multiple_of(i * row_count // 2, row_count // 2), row_count // 2)
        for b in range(pb_count):
            at = (b % 2) * half + b // 2
            wt[cols, at * share:(at + 1) * share] = w[b * share:(b + 1) * share, cols].T

    w_copy.wait()
    steps = point_total * 2 // row_count
    turn_w(0)
    spread(0, 0)
    loop(1, steps // 2, turn_w)
    spread(0, 1)
    send(1)
    turn_w(steps // 2)
    spread(0, 2)
    loop(steps // 2 + 1, steps - 2, turn_w)
    pass_far(0, 0)
    send(2)
    loop(steps - 2, steps, turn_w)
    pass_far(0, 1)
    for p in range(3, pair_total):
        send(p)
    pass_far(0, 2)
    spread(1, 0)

    def tile_t(p, at, side):
        lanes = slice(side * width, (side + 1) * width)
        return jnp.concatenate([basis[p, r, m, lanes, :] for m in at for r in range(row_devices)], axis=1)

    def finish(p):
        fold(p, 1).wait_recv()
        shed(p).wait_recv()
        total = keep[p, 1] + l1r[p, 1] + l2r[p].astype(F32)
        for j in range(pb_count):
            cbuf[p, 1, j] = total[:, j * share:(j + 1) * share].astype(BF16)
        for dz in range(1, half):
            give(p, 1, dz, 0).start()
            give(p, 1, dz, 1).start()
        give(p, 1, 0, 1 - side_x).start()
        own_c(p, 1).start()

    def column_tile(p, n):
        s = order[n]
        cols = pl.ds(pl.multiple_of(s * row_count, row_count), row_count)
        there_l, there_r = tile_t(p, order_slots[n], 0), tile_t(p, order_slots[n], 1)
        nat_r[p % 2, s] = there_r.T
        total = None
        chunk = row_count // 2
        for m in range(2):
            here = slice(m * chunk, (m + 1) * chunk)
            gram = jnp.dot(rows_l[here], there_l, preferred_element_type=F32)
            term = jnp.dot(rows_r[:, here], (w[here, cols].astype(F32) * gram).astype(BF16), preferred_element_type=F32)
            total = term if total is None else total + term
        return total

    def row_tile(p, h, s):
        lanes = slice(h * row_count // 2, (h + 1) * row_count // 2)
        gram = jnp.dot(nat_r[p % 2, s], rows_p[p % 2, :, lanes], preferred_element_type=F32)
        rows = slice(s * row_count, (s + 1) * row_count)
        return jnp.dot(tile_t(p, slots[s], 0), (wt[rows, lanes].astype(F32) * gram).astype(BF16), preferred_element_type=F32)

    def columns(p, after):
        for g in groups:
            to_mate(p, g).wait_recv()
            onward(p, g).wait_recv()
        rows_l[...] = tile_t(p, order_slots[3], 0).T
        right = tile_t(p, order_slots[3], 1)
        rows_r[...] = right
        spun = [b for h in range(2) for b in range(h, pb_count, 2)]
        rows_p[p % 2] = jnp.concatenate([right[:, b * share:(b + 1) * share] for b in spun], axis=1)
        l1s[p, 0] = column_tile(p, 0)
        after(0)
        keep[p, 0] = column_tile(p, 1)
        fold(p, 0).start()
        after(1)
        l1s[p, 1] = column_tile(p, 2)
        fold(p, 1).start()
        fold(p, 0).wait_recv()
        l2s[p] = (keep[p, 0] + l1r[p, 0]).astype(BF16)
        shed(p).start()
        after(2)
        keep[p, 1] = column_tile(p, 3)
        after(3)

    def rows(p, after):
        for h in range(2):
            total = None
            for s in range(row_devices):
                term = row_tile(p, h, s)
                total = term if total is None else total + term
                if s == 1:
                    after(2 * h)
            for i in range(half):
                cbuf[p, 0, 2 * i + h] = total[:, i * share:(i + 1) * share].astype(BF16)
            for dz in range(1, half):
                give(p, 0, dz, h).start()
            if h == 1:
                give(p, 0, 0, 1 - side_x).start()
                own_c(p, 0).start()
            after(2 * h + 1)

    top = pair_total - 1
    serves = {}

    def at(unit, p, point, act, *which):
        serves.setdefault((unit, p, point), []).append(lambda: act(*which))

    at(columns, 0, 0, spread, 1, 1)
    at(columns, 0, 1, spread, 1, 2)
    for p in range(2, pair_total):
        if p < top:
            at(rows, p - 2, 3, spread, p, 0)
            at(columns, p - 1, 0, spread, p, 1)
            at(columns, p - 1, 1, spread, p, 2)
    for p in range(1, top):
        for g in groups:
            at(rows, p - 1, g, pass_far, p, g)
    for g in groups:
        at(rows, top - 2, g, spread, top, g)
        at(columns, top - 1, g + 1, pass_far, top, g)
    for p in range(top - 1):
        at(columns, p + 1, 2 if p == 0 else 0, finish, p)
    at(rows, top - 1, 3, finish, top - 1)
    at(rows, top, 2, finish, top)

    def run(unit, p):
        unit(p, lambda point: [act() for act in serves.get((unit, p, point), ())])

    for p in range(pair_total):
        run(columns, p)
        run(rows, p)

    def sent(ref, sem):
        pltpu.make_async_copy(ref, ref, sem).wait()

    for sem in (x_send, g_send, h_send):
        sent(basis.at[:, 0, pl.ds(1, pb_count - 1)], sem)
    sent(picked.at[:, pl.ds(1, pb_count - 1)], d_send)
    sent(l1s, a_send)
    sent(l2s, b_send)
    sent(cbuf.at[:, :, pl.ds(1, pb_count - 1)], c_send)
    sent(cbuf.at[:, :, 0], own_sem)
    arrived = out.at[:, :, pl.ds(1, pb_count - 1)]
    sent(arrived, c_recv)


def swift_combine(pairs_ref, count_ref, got_ref, out_ref, total):
    pair_total, sides, pb_count, width, share = got_ref.shape
    total[...] = jnp.zeros_like(total)

    def step(q, carry):
        for p in range(pair_total):
            live = p < count_ref[q]
            for side in range(sides):
                k = pairs_ref[p, side, q]
                total[k] += jnp.where(live, got_ref[p, side, q].astype(F32), 0.0)
        return carry

    lax.fori_loop(0, pb_count, step, 0)
    out_ref[0] = total[...].reshape(total.shape[0] * width, share).T


def swift_shards(kernels, orbitals, pairs, k_slot, pair_count):
    pb_count, row_devices = lax.axis_size("pb"), lax.axis_size("row")
    row_count, point_total = kernels.shape[1:]
    pair_total = pairs.shape[1]
    k_total = k_slot.shape[0]
    width = orbitals.shape[1] // k_total
    piece = orbitals.shape[0] // row_devices
    share = row_count // pb_count
    pairs = jnp.transpose(pairs, (1, 2, 0))
    smem = pl.BlockSpec(memory_space=pltpu.SMEM)
    vmem = pl.BlockSpec(memory_space=pltpu.VMEM)
    hbm = pl.BlockSpec(memory_space=pl.ANY)
    sems = pltpu.SemaphoreType.DMA
    got = pl.pallas_call(
        functools.partial(swift_kernel, (pb_count, pair_total, piece, width)),
        out_shape=jax.ShapeDtypeStruct((pair_total, 2, pb_count, width, share), BF16),
        in_specs=[smem, smem, hbm, hbm],
        out_specs=hbm,
        scratch_shapes=[
            pltpu.VMEM(orbitals.shape, BF16),
            pltpu.VMEM((row_devices, k_total, width, piece), BF16),
            pltpu.VMEM((row_count, point_total), BF16),
            pltpu.VMEM((point_total, row_count), BF16),
            pltpu.VMEM((pair_total, pb_count, 2 * width, piece), BF16),
            pltpu.VMEM((pair_total, row_devices, pb_count, 2 * width, piece), BF16),
            pltpu.VMEM((row_count, width), BF16),
            pltpu.VMEM((width, row_count), BF16),
            pltpu.VMEM((2, width, row_count), BF16),
            pltpu.VMEM((2, row_devices, row_count, width), BF16),
            pltpu.VMEM((pair_total, 2, width, row_count), F32),
            pltpu.VMEM((pair_total, 2, width, row_count), F32),
            pltpu.VMEM((pair_total, 2, width, row_count), F32),
            pltpu.VMEM((pair_total, width, row_count), BF16),
            pltpu.VMEM((pair_total, width, row_count), BF16),
            pltpu.VMEM((pair_total, 2, pb_count, width, share), BF16),
            sems,
            sems,
            sems,
            sems((pair_total, 3)),
            sems,
            sems((pair_total, 3)),
            sems,
            sems((pair_total, 3)),
            sems,
            sems((pair_total, 3)),
            sems,
            sems((pair_total, 2)),
            sems,
            sems((pair_total,)),
            sems,
            sems,
            sems,
        ],
        compiler_params=pltpu.CompilerParams(
            collective_id=1, has_side_effects=True, vmem_limit_bytes=60 * 1024 * 1024
        ),
    )(pairs, k_slot, orbitals, kernels)
    return pl.pallas_call(
        swift_combine,
        out_shape=jax.ShapeDtypeStruct((1, share, k_total * width), F32),
        in_specs=[smem, smem, vmem],
        out_specs=vmem,
        scratch_shapes=[pltpu.VMEM((k_total, width, share), F32)],
    )(pairs, pair_count, got)


def shards(kernels, orbitals, pairs, k_slot, pair_count):
    pb_count, row_devices = lax.axis_size("pb"), lax.axis_size("row")
    piece = orbitals.shape[0] // row_devices
    share = kernels.shape[1] // pb_count
    width = orbitals.shape[1] // k_slot.shape[0]
    whole_tiles = piece % 128 == 0 and share % 128 == 0 and width % 16 == 0
    paired = row_devices == 4 and pb_count % row_devices == 0 and pb_count >= 8 and pairs.shape[1] > 2
    form = swift_shards if whole_tiles and paired else plain_shards
    return form(kernels, orbitals, pairs, k_slot, pair_count)


def solution(mesh):
    placed = (P("pb", "row", None), P("pb", None), P(), P(), P())
    return jax.shard_map(
        shards, mesh=mesh, in_specs=placed, out_specs=P("row", "pb", None), check_vma=False
    )
```

```python
import functools

import jax
import jax.numpy as jnp
from jax import lax
from jax.experimental import pallas as pl
from jax.experimental.pallas import tpu as pltpu
from jax.sharding import PartitionSpec as P

MESH = pl.DeviceIdType.MESH
BF16 = jnp.bfloat16
F32 = jnp.float32
NT = (((1,), (1,)), ((), ()))


def pick_kernel(width, pairs_ref, slot_ref, orb_ref, out_ref):
    pair_total, pb_count, piece, lanes = out_ref.shape
    rows = pl.ds(pl.multiple_of(lax.axis_index("row") * piece, piece), piece)
    low = lax.broadcasted_iota(jnp.int32, (piece, lanes), 1) < width

    def fetch(k, want):
        slot = slot_ref[k]
        block = orb_ref[rows, pl.ds(pl.multiple_of((slot >> 1) * lanes, lanes), lanes)].astype(F32)
        moved = pltpu.roll(block, width, 1)
        return jnp.where((slot & 1) == want, block, moved)

    def step(q, carry):
        for p in range(pair_total):
            left = fetch(pairs_ref[q, p, 0], 0)
            right = fetch(pairs_ref[q, p, 1], 1)
            out_ref[p, q] = jnp.where(low, left, right).astype(BF16)
        return carry

    lax.fori_loop(0, pb_count, step, 0)


def main_kernel(dims, picked, kern, out, w, basis, rows_r, rows_l, rows_t, f1, f2s, f2r, cbuf,
                w_sem, d_send, d_recv, g_send, g_recv, h_send, h_recv, y_send, y_recv,
                s_send, s_recv, c_send, c_recv):
    pb_count, row_devices, pair_total, piece, width = dims
    pb, row = lax.axis_index("pb"), lax.axis_index("row")
    chips = row_devices // 2
    part, chip = lax.rem(row, 2), lax.div(row, 2)
    mate = row + 1 - 2 * part
    row_count = w.shape[0]
    lanes = basis.shape[4]
    share = row_count // pb_count
    order = [(e, flip) for e in range(1, chips) for flip in (0, 1)] + [(0, 1), (0, 0)]

    def peer(e, flip):
        side = 1 - part if flip else part
        return 2 * lax.rem(chip + e, chips) + side

    w_copy = pltpu.make_async_copy(kern.at[0], w, w_sem)
    w_copy.start()

    barrier = pltpu.get_barrier_semaphore()

    def greet_pb(d, c):
        pl.semaphore_signal(barrier, inc=1, device_id=(lax.rem(pb + d, pb_count), row), device_id_type=MESH)
        return c

    def greet_row(d, c):
        pl.semaphore_signal(barrier, inc=1, device_id=(pb, lax.rem(row + d, row_devices)), device_id_type=MESH)
        return c

    lax.fori_loop(1, pb_count, greet_pb, 0)
    lax.fori_loop(1, row_devices, greet_row, 0)
    pl.semaphore_wait(barrier, pb_count + row_devices - 2)

    def spot(p, j, which):
        return basis.at[p, j, which]

    def points(p, r):
        span = pb_count // row_devices
        return basis[p, pl.ds(r * span, span)].reshape(row_count, lanes)

    def own(p):
        return pltpu.make_async_copy(picked.at[p, pb], spot(p, pb, row), d_recv.at[p, 0])

    def direct(p, d):
        q = lax.rem(pb + d, pb_count)
        return pltpu.make_async_remote_copy(
            src_ref=picked.at[p, q], dst_ref=spot(p, pb, row),
            send_sem=d_send.at[p, d], recv_sem=d_recv.at[p, d],
            device_id=(q, row), device_id_type=MESH)

    def across(p, e):
        block = basis.at[p, :, row]
        return pltpu.make_async_remote_copy(
            src_ref=block, dst_ref=block, send_sem=y_send.at[p, e - 1], recv_sem=y_recv.at[p, e - 1],
            device_id=(pb, peer(e, 0)), device_id_type=MESH)

    def to_mate(p):
        block = basis.at[p, :, row]
        return pltpu.make_async_remote_copy(
            src_ref=block, dst_ref=block, send_sem=g_send.at[p], recv_sem=g_recv.at[p],
            device_id=(pb, mate), device_id_type=MESH)

    def onward(p, e):
        block = basis.at[p, :, peer(chips - e, 0)]
        return pltpu.make_async_remote_copy(
            src_ref=block, dst_ref=block, send_sem=h_send.at[p, e - 1], recv_sem=h_recv.at[p, e - 1],
            device_id=(pb, mate), device_id_type=MESH)

    def shed(p, s):
        to = peer(*order[s])
        return pltpu.make_async_remote_copy(
            src_ref=f2s.at[p, s], dst_ref=f2r.at[p, s], send_sem=s_send.at[p, s], recv_sem=s_recv.at[p, s],
            device_id=(pb, to), device_id_type=MESH)

    def c_rows(j):
        return pl.ds(pl.multiple_of(j * share, share), share)

    def own_c(p):
        return pltpu.make_async_copy(cbuf.at[p, c_rows(pb)], out.at[p, pb], c_recv.at[p, 0])

    def give(p, d):
        j = lax.rem(pb + d, pb_count)
        return pltpu.make_async_remote_copy(
            src_ref=cbuf.at[p, c_rows(j)], dst_ref=out.at[p, pb], send_sem=c_send.at[p, d], recv_sem=c_recv.at[p, d],
            device_id=(j, row), device_id_type=MESH)

    def loop(low, high, body):
        def step(i, c):
            body(i)
            return c
        lax.fori_loop(low, high, step, 0)

    def send_pair(p):
        own(p).start()
        loop(1, pb_count, lambda d: direct(p, d).start())

    loop(0, pair_total, send_pair)

    def spread(p):
        own(p).wait()
        loop(1, pb_count, lambda d: direct(p, d).wait_recv())
        for e in range(1, chips):
            across(p, e).start()
        to_mate(p).start()

    def pass_far(p):
        for e in range(1, chips):
            across(p, e).wait_recv()
            onward(p, e).start()

    low = lax.broadcasted_iota(jnp.int32, (row_count, lanes), 1) < width

    def finish_pair(p):
        total = f2s[p, row_devices - 1].astype(F32)
        for s in range(row_devices - 1):
            shed(p, s).wait_recv()
            total = total + f2r[p, s].astype(F32)
        stacked = jnp.concatenate([jnp.zeros_like(total), total], axis=0)
        cbuf[p] = jnp.where(low, f1[p], stacked.T).astype(BF16)
        loop(1, pb_count, lambda d: give(p, d).start())
        own_c(p).start()

    def tile_of(p, s):
        to = peer(*order[s])
        cols = pl.ds(pl.multiple_of(to * row_count, row_count), row_count)
        there = points(p, to)
        second = None
        chunk = row_count // 2
        for m in range(2):
            here = slice(m * chunk, (m + 1) * chunk)
            weight = w[here, cols].astype(F32)
            gram = lax.dot_general(rows_r[here], there, NT, preferred_element_type=F32)
            first = jnp.dot((weight * gram).astype(BF16), there, preferred_element_type=F32)
            f1[p, here] = first if s == 0 else f1[p, here] + first
            gram = lax.dot_general(rows_l[here], there, NT, preferred_element_type=F32)
            term = jnp.dot(rows_t[:, here], (weight * gram).astype(BF16), preferred_element_type=F32)
            second = term if second is None else second + term
        f2s[p, s] = second[width:].astype(BF16)
        if s < row_devices - 1:
            shed(p, s).start()

    spread(0)
    pass_far(0)
    w_copy.wait()

    def pair_step(p):
        to_mate(p).wait_recv()
        for e in range(1, chips):
            onward(p, e).wait_recv()
        mine = points(p, row).astype(F32)
        rows_r[...] = jnp.where(low, 0, mine).astype(BF16)
        rows_l[...] = jnp.where(low, mine, 0).astype(BF16)
        rows_t[...] = mine.T.astype(BF16)
        for s in range(row_devices):
            tile_of(p, s)
            if s == 0:
                pl.when(p + 1 < pair_total)(lambda: spread(p + 1))
                pl.when(p > 0)(lambda: finish_pair(p - 1))
            if s == row_devices - 2:
                pl.when(p + 1 < pair_total)(lambda: pass_far(p + 1))

    loop(0, pair_total, pair_step)
    finish_pair(pair_total - 1)

    def settle(p):
        own_c(p).wait()

        to_mate(p).wait_send()
        for e in range(1, chips):
            across(p, e).wait_send()
            onward(p, e).wait_send()

        def one(d):
            direct(p, d).wait_send()
            give(p, d).wait()

        loop(1, pb_count, one)
        for s in range(row_devices - 1):
            shed(p, s).wait_send()

    loop(0, pair_total, settle)


def combine_kernel(width, pairs_ref, count_ref, got_ref, out_ref):
    pair_total, pb_count, share, lanes = got_ref.shape
    low = lax.broadcasted_iota(jnp.int32, (share, lanes), 1) < width
    out_ref[...] = jnp.zeros_like(out_ref)

    def step(q, carry):
        for p in range(pair_total):
            live = p < count_ref[q]
            block = jnp.where(live, got_ref[p, q].astype(F32), 0.0)
            moved = pltpu.roll(block, width, 1)
            for side in range(2):
                k = pairs_ref[q, p, side]
                odd = k & 1
                value = jnp.where(odd == side, block, moved)
                value = jnp.where(low == (odd == 0), value, 0.0)
                spot = pl.ds(pl.multiple_of((k >> 1) * lanes, lanes), lanes)
                out_ref[0, :, spot] += value
        return carry

    lax.fori_loop(0, pb_count, step, 0)


def plain_shards(kernels, orbitals, pairs, k_slot, pair_count):
    pb_count, row_devices = lax.axis_size("pb"), lax.axis_size("row")
    row_count, point_total = kernels.shape[1:]
    pair_total = pairs.shape[1]
    k_total = k_slot.shape[0]
    width = orbitals.shape[1] // k_total
    lanes = 2 * width
    piece = orbitals.shape[0] // row_devices
    far = max(row_devices // 2 - 1, 1)
    share = row_count // pb_count
    smem = pl.BlockSpec(memory_space=pltpu.SMEM)
    vmem = pl.BlockSpec(memory_space=pltpu.VMEM)
    hbm = pl.BlockSpec(memory_space=pl.ANY)
    picked = pl.pallas_call(
        functools.partial(pick_kernel, width),
        out_shape=jax.ShapeDtypeStruct((pair_total, pb_count, piece, lanes), BF16),
        in_specs=[smem, smem, vmem],
        out_specs=vmem,
    )(pairs, k_slot, orbitals)
    sems = pltpu.SemaphoreType.DMA
    got = pl.pallas_call(
        functools.partial(main_kernel, (pb_count, row_devices, pair_total, piece, width)),
        out_shape=jax.ShapeDtypeStruct((pair_total, pb_count, share, lanes), BF16),
        in_specs=[hbm, hbm],
        out_specs=hbm,
        scratch_shapes=[
            pltpu.VMEM((row_count, point_total), BF16),
            pltpu.VMEM((pair_total, pb_count, row_devices, piece, lanes), BF16),
            pltpu.VMEM((row_count, lanes), BF16),
            pltpu.VMEM((row_count, lanes), BF16),
            pltpu.VMEM((lanes, row_count), BF16),
            pltpu.VMEM((pair_total, row_count, lanes), F32),
            pltpu.VMEM((pair_total, row_devices, width, row_count), BF16),
            pltpu.VMEM((pair_total, row_devices, width, row_count), BF16),
            pltpu.VMEM((pair_total, row_count, lanes), BF16),
            sems,
            sems((pair_total, pb_count)),
            sems((pair_total, pb_count)),
            sems((pair_total,)),
            sems((pair_total,)),
            sems((pair_total, far)),
            sems((pair_total, far)),
            sems((pair_total, far)),
            sems((pair_total, far)),
            sems((pair_total, row_devices)),
            sems((pair_total, row_devices)),
            sems((pair_total, pb_count)),
            sems((pair_total, pb_count)),
        ],
        compiler_params=pltpu.CompilerParams(
            collective_id=0, has_side_effects=True, vmem_limit_bytes=56 * 1024 * 1024
        ),
    )(picked, kernels)
    return pl.pallas_call(
        functools.partial(combine_kernel, width),
        out_shape=jax.ShapeDtypeStruct((1, share, k_total * width), F32),
        in_specs=[smem, smem, vmem],
        out_specs=vmem,
    )(pairs, pair_count, got)


def swift_kernel(dims, pairs_ref, slot_ref, orb, kern, out, orb_v, orb_t, w, wt, picked, basis, rows_l, rows_r,
                 rows_p, nat_r, l1s, l1r, keep, l2s, l2r, cbuf, o_sem, w_sem, d_send, d_recv, x_send, x_recv,
                 g_send, g_recv, h_send, h_recv, a_send, a_recv, b_send, b_recv, c_send, c_recv, own_sem):
    pb_count, pair_total, piece, width = dims
    pb, row = lax.axis_index("pb"), lax.axis_index("row")
    row_devices = basis.shape[1]
    row_count, point_total = w.shape
    span = pb_count // row_devices
    half = pb_count // 2
    share = row_count // pb_count
    part, chip = lax.rem(row, 2), lax.div(row, 2)
    side_x, side_z = lax.rem(pb, 2), lax.div(pb, 2)
    mate = row + 1 - 2 * part
    far = 2 * (1 - chip) + part
    bounds = [1, half, half + half // 2, pb_count]
    groups = range(3)
    group_of = [0] + [g for g in groups for m in range(bounds[g], bounds[g + 1])]

    turned = [side_x, 1 - side_x]
    ahead = [lax.rem(side_z + m // 2, half) * 2 + turned[m % 2] for m in range(pb_count)]

    def slots_of(s):
        picks = []
        for i in range(span):
            j = s * span + i
            dz = lax.rem(side_z - lax.div(j, 2) + half, half)
            picks.append(2 * dz + lax.rem(side_x + j, 2))
        return picks

    slots = [slots_of(jnp.int32(s)) for s in range(row_devices)]
    diagonal = 2 * (1 - chip) + 1 - part
    order = [diagonal, far, mate, row]
    order_slots = [slots_of(s) for s in order]
    others = range(1, pb_count)

    def loop(low, high, body):
        def step(i, c):
            body(i)
            return c
        lax.fori_loop(low, high, step, 0)

    orb_copy = pltpu.make_async_copy(orb, orb_v, o_sem)
    orb_copy.start()
    w_copy = pltpu.make_async_copy(kern.at[0], w, w_sem)
    w_copy.start()

    barrier = pltpu.get_barrier_semaphore()
    loop(1, pb_count, lambda m: pl.semaphore_signal(
        barrier, inc=1, device_id=(lax.rem(pb + m, pb_count), row), device_id_type=MESH))
    pl.semaphore_signal(barrier, inc=1, device_id=(pb, mate), device_id_type=MESH)
    pl.semaphore_signal(barrier, inc=1, device_id=(pb, far), device_id_type=MESH)

    def direct(p, m):
        return pltpu.make_async_remote_copy(
            src_ref=picked.at[p, m], dst_ref=basis.at[p, row, m],
            send_sem=d_send, recv_sem=d_recv.at[p, group_of[m]],
            device_id=(ahead[m], row), device_id_type=MESH)

    def passed(p, g, quarter, to, send, recv):
        block = basis.at[p, quarter, pl.ds(bounds[g], bounds[g + 1] - bounds[g])]
        return pltpu.make_async_remote_copy(
            src_ref=block, dst_ref=block, send_sem=send, recv_sem=recv.at[p, g],
            device_id=(pb, to), device_id_type=MESH)

    def across(p, g):
        return passed(p, g, row, far, x_send, x_recv)

    def to_mate(p, g):
        return passed(p, g, row, mate, g_send, g_recv)

    def onward(p, g):
        return passed(p, g, far, mate, h_send, h_recv)

    def fold(p, i):
        return pltpu.make_async_remote_copy(
            src_ref=l1s.at[p, i], dst_ref=l1r.at[p, i], send_sem=a_send, recv_sem=a_recv.at[p, i],
            device_id=(pb, mate), device_id_type=MESH)

    def shed(p):
        return pltpu.make_async_remote_copy(
            src_ref=l2s.at[p], dst_ref=l2r.at[p], send_sem=b_send, recv_sem=b_recv.at[p],
            device_id=(pb, far), device_id_type=MESH)

    def give(p, side, dz, x):
        to = 2 * lax.rem(side_z + dz, half) + x
        return pltpu.make_async_remote_copy(
            src_ref=cbuf.at[p, side, to], dst_ref=out.at[p, side, pb],
            send_sem=c_send, recv_sem=c_recv, device_id=(to, row), device_id_type=MESH)

    def own_c(p, side):
        return pltpu.make_async_copy(cbuf.at[p, side, pb], out.at[p, side, pb], own_sem)

    def take(quarter, k):
        return orb_t[quarter, slot_ref[k]]

    orb_copy.wait()

    def turn(r):
        block = orb_v[pl.ds(pl.multiple_of(r * piece, piece), piece), :].T
        orb_t[r] = block.reshape(orb_t.shape[1:])

    turn(row)

    def pick(p):
        for m in others:
            for side in range(2):
                picked[p, m, side * width:(side + 1) * width] = take(row, pairs_ref[p, side, ahead[m]])

    def send(p):
        for m in others:
            direct(p, m).start()

    pick(0)
    pl.semaphore_wait(barrier, pb_count + 1)
    send(0)

    loop(1, pair_total, pick)
    loop(1, row_devices, lambda e: turn(lax.rem(row + e, row_devices)))

    def own(p):
        def one(r):
            for side in range(2):
                basis[p, r, 0, side * width:(side + 1) * width] = take(r, pairs_ref[p, side, pb])
        loop(0, row_devices, one)

    loop(0, pair_total, own)

    def spread(p, *which):
        for g in which:
            arrived = basis.at[p, row, pl.ds(bounds[g], bounds[g + 1] - bounds[g])]
            pltpu.make_async_copy(arrived, arrived, d_recv.at[p, g]).wait()
            across(p, g).start()
            to_mate(p, g).start()

    def pass_far(p, *which):
        for g in which:
            across(p, g).wait_recv()
            onward(p, g).start()

    def turn_w(i):
        cols = pl.ds(pl.multiple_of(i * row_count // 2, row_count // 2), row_count // 2)
        for b in range(pb_count):
            at = (b % 2) * half + b // 2
            wt[cols, at * share:(at + 1) * share] = w[b * share:(b + 1) * share, cols].T

    steps = point_total * 2 // row_count
    spread(0, 0)
    w_copy.wait()
    loop(0, steps // 2, turn_w)
    spread(0, 1)
    send(1)
    turn_w(steps // 2)
    spread(0, 2)
    loop(steps // 2 + 1, steps - 2, turn_w)
    pass_far(0, 0)
    send(2)
    loop(steps - 2, steps, turn_w)
    pass_far(0, 1)
    for p in range(3, pair_total):
        send(p)
    pass_far(0, 2)
    spread(1, 0)

    def tile_t(p, at, side):
        lanes = slice(side * width, (side + 1) * width)
        return jnp.concatenate([basis[p, r, m, lanes, :] for m in at for r in range(row_devices)], axis=1)

    def finish(p):
        fold(p, 1).wait_recv()
        shed(p).wait_recv()
        total = keep[p, 1] + l1r[p, 1].astype(F32) + l2r[p].astype(F32)
        for j in range(pb_count):
            cbuf[p, 1, j] = total[:, j * share:(j + 1) * share].astype(BF16)
        for dz in range(1, half):
            give(p, 1, dz, 0).start()
            give(p, 1, dz, 1).start()
        give(p, 1, 0, 1 - side_x).start()
        own_c(p, 1).start()

    def column_tile(p, n):
        s = order[n]
        cols = pl.ds(pl.multiple_of(s * row_count, row_count), row_count)
        there_l, there_r = tile_t(p, order_slots[n], 0), tile_t(p, order_slots[n], 1)
        nat_r[p % 2, s] = there_r.T
        total = None
        chunk = row_count // 2
        for m in range(2):
            here = slice(m * chunk, (m + 1) * chunk)
            gram = jnp.dot(rows_l[here], there_l, preferred_element_type=F32)
            term = jnp.dot(rows_r[:, here], (w[here, cols].astype(F32) * gram).astype(BF16), preferred_element_type=F32)
            total = term if total is None else total + term
        return total

    def row_tile(p, h, s):
        lanes = slice(h * row_count // 2, (h + 1) * row_count // 2)
        gram = jnp.dot(nat_r[p % 2, s], rows_p[p % 2, :, lanes], preferred_element_type=F32)
        rows = slice(s * row_count, (s + 1) * row_count)
        return jnp.dot(tile_t(p, slots[s], 0), (wt[rows, lanes].astype(F32) * gram).astype(BF16), preferred_element_type=F32)

    def columns(p, after):
        for g in groups:
            to_mate(p, g).wait_recv()
            onward(p, g).wait_recv()
        rows_l[...] = tile_t(p, order_slots[3], 0).T
        right = tile_t(p, order_slots[3], 1)
        rows_r[...] = right
        spun = [b for h in range(2) for b in range(h, pb_count, 2)]
        rows_p[p % 2] = jnp.concatenate([right[:, b * share:(b + 1) * share] for b in spun], axis=1)
        l1s[p, 0] = column_tile(p, 0).astype(BF16)
        after(0)
        keep[p, 0] = column_tile(p, 1)
        fold(p, 0).start()
        after(1)
        l1s[p, 1] = column_tile(p, 2).astype(BF16)
        fold(p, 1).start()
        fold(p, 0).wait_recv()
        l2s[p] = (keep[p, 0] + l1r[p, 0].astype(F32)).astype(BF16)
        shed(p).start()
        after(2)
        keep[p, 1] = column_tile(p, 3)
        after(3)

    def rows(p, after):
        for h in range(2):
            total = None
            for s in range(row_devices):
                term = row_tile(p, h, s)
                total = term if total is None else total + term
                if s == 1:
                    after(2 * h)
            for i in range(half):
                cbuf[p, 0, 2 * i + h] = total[:, i * share:(i + 1) * share].astype(BF16)
            for dz in range(1, half):
                give(p, 0, dz, h).start()
            if h == 1:
                give(p, 0, 0, 1 - side_x).start()
                own_c(p, 0).start()
            after(2 * h + 1)

    top = pair_total - 1
    serves = {}

    def at(unit, p, point, act, *which):
        serves.setdefault((unit, p, point), []).append(lambda: act(*which))

    at(columns, 0, 0, spread, 1, 1)
    at(columns, 0, 1, spread, 1, 2)
    for p in range(2, pair_total):
        if p < top:
            at(rows, p - 2, 3, spread, p, 0)
            at(columns, p - 1, 0, spread, p, 1)
            at(columns, p - 1, 1, spread, p, 2)
    for p in range(1, top):
        for g in groups:
            at(rows, p - 1, g, pass_far, p, g)
    for g in groups:
        at(rows, top - 2, g, spread, top, g)
        at(columns, top - 1, g + 1, pass_far, top, g)
    for p in range(top - 1):
        at(columns, p + 1, 2 if p == 0 else 0, finish, p)
    at(rows, top - 1, 3, finish, top - 1)
    at(rows, top, 2, finish, top)

    def run(unit, p):
        unit(p, lambda point: [act() for act in serves.get((unit, p, point), ())])

    for p in range(pair_total):
        run(columns, p)
        run(rows, p)

    def sent(ref, sem):
        pltpu.make_async_copy(ref, ref, sem).wait()

    for sem in (x_send, g_send, h_send):
        sent(basis.at[:, 0, pl.ds(1, pb_count - 1)], sem)
    sent(picked.at[:, pl.ds(1, pb_count - 1)], d_send)
    sent(l1s, a_send)
    sent(l2s, b_send)
    sent(cbuf.at[:, :, pl.ds(1, pb_count - 1)], c_send)
    sent(cbuf.at[:, :, 0], own_sem)
    arrived = out.at[:, :, pl.ds(1, pb_count - 1)]
    sent(arrived, c_recv)


def swift_combine(pairs_ref, count_ref, got_ref, out_ref, total):
    pair_total, sides, pb_count, width, share = got_ref.shape
    total[...] = jnp.zeros_like(total)

    def step(q, carry):
        for p in range(pair_total):
            live = p < count_ref[q]
            for side in range(sides):
                k = pairs_ref[p, side, q]
                total[k] += jnp.where(live, got_ref[p, side, q].astype(F32), 0.0)
        return carry

    lax.fori_loop(0, pb_count, step, 0)
    out_ref[0] = total[...].reshape(total.shape[0] * width, share).T


def swift_shards(kernels, orbitals, pairs, k_slot, pair_count):
    pb_count, row_devices = lax.axis_size("pb"), lax.axis_size("row")
    row_count, point_total = kernels.shape[1:]
    pair_total = pairs.shape[1]
    k_total = k_slot.shape[0]
    width = orbitals.shape[1] // k_total
    piece = orbitals.shape[0] // row_devices
    share = row_count // pb_count
    pairs = jnp.transpose(pairs, (1, 2, 0))
    smem = pl.BlockSpec(memory_space=pltpu.SMEM)
    vmem = pl.BlockSpec(memory_space=pltpu.VMEM)
    hbm = pl.BlockSpec(memory_space=pl.ANY)
    sems = pltpu.SemaphoreType.DMA
    got = pl.pallas_call(
        functools.partial(swift_kernel, (pb_count, pair_total, piece, width)),
        out_shape=jax.ShapeDtypeStruct((pair_total, 2, pb_count, width, share), BF16),
        in_specs=[smem, smem, hbm, hbm],
        out_specs=hbm,
        scratch_shapes=[
            pltpu.VMEM(orbitals.shape, BF16),
            pltpu.VMEM((row_devices, k_total, width, piece), BF16),
            pltpu.VMEM((row_count, point_total), BF16),
            pltpu.VMEM((point_total, row_count), BF16),
            pltpu.VMEM((pair_total, pb_count, 2 * width, piece), BF16),
            pltpu.VMEM((pair_total, row_devices, pb_count, 2 * width, piece), BF16),
            pltpu.VMEM((row_count, width), BF16),
            pltpu.VMEM((width, row_count), BF16),
            pltpu.VMEM((2, width, row_count), BF16),
            pltpu.VMEM((2, row_devices, row_count, width), BF16),
            pltpu.VMEM((pair_total, 2, width, row_count), BF16),
            pltpu.VMEM((pair_total, 2, width, row_count), BF16),
            pltpu.VMEM((pair_total, 2, width, row_count), F32),
            pltpu.VMEM((pair_total, width, row_count), BF16),
            pltpu.VMEM((pair_total, width, row_count), BF16),
            pltpu.VMEM((pair_total, 2, pb_count, width, share), BF16),
            sems,
            sems,
            sems,
            sems((pair_total, 3)),
            sems,
            sems((pair_total, 3)),
            sems,
            sems((pair_total, 3)),
            sems,
            sems((pair_total, 3)),
            sems,
            sems((pair_total, 2)),
            sems,
            sems((pair_total,)),
            sems,
            sems,
            sems,
        ],
        compiler_params=pltpu.CompilerParams(
            collective_id=1, has_side_effects=True, vmem_limit_bytes=60 * 1024 * 1024
        ),
    )(pairs, k_slot, orbitals, kernels)
    return pl.pallas_call(
        swift_combine,
        out_shape=jax.ShapeDtypeStruct((1, share, k_total * width), F32),
        in_specs=[smem, smem, vmem],
        out_specs=vmem,
        scratch_shapes=[pltpu.VMEM((k_total, width, share), F32)],
    )(pairs, pair_count, got)


def shards(kernels, orbitals, pairs, k_slot, pair_count):
    pb_count, row_devices = lax.axis_size("pb"), lax.axis_size("row")
    piece = orbitals.shape[0] // row_devices
    share = kernels.shape[1] // pb_count
    width = orbitals.shape[1] // k_slot.shape[0]
    whole_tiles = piece % 128 == 0 and share % 128 == 0 and width % 16 == 0
    paired = row_devices == 4 and pb_count % row_devices == 0 and pb_count >= 8 and pairs.shape[1] > 2
    form = swift_shards if whole_tiles and paired else plain_shards
    return form(kernels, orbitals, pairs, k_slot, pair_count)


def solution(mesh):
    placed = (P("pb", "row", None), P("pb", None), P(), P(), P())
    return jax.shard_map(
        shards, mesh=mesh, in_specs=placed, out_specs=P("row", "pb", None), check_vma=False
    )
```
